32 devices in a mesh: section: 16 (over z, y, x), expert: 2 (over core).
Axes of the slice: x: 2, y: 2, z: 4, core: 2. Of those that a mesh axis runs over, the one named last changes fastest.
Arguments:
- incoming: bfloat16 [2048, 4096], P('section', 'expert'), may hold values from -26 to 26
- expert_ids: int32 [4, 2048, 2], P(None, 'section'), may hold values from 0 to 7, all different within a row; in each aligned block of 128 rows (0 to 127, 128 to 255, ..., all dimensions but the last counted through in order) at most 40 rows name the same one
- gates: float32 [4, 2048, 2], P(None, 'section'), may hold values from 0 to 1, as said below
- pre_act: bfloat16 [4, 5120, 16], P(None, ('section', 'expert')), may hold values from -8 to 8
- w_up: bfloat16 [128, 16, 4096], P(('section', 'expert')), may hold values from -0.09375 to 0.09375
- w_down: bfloat16 [128, 16, 4096], P(('section', 'expert')), may hold values from -1.5 to 1.5
- delta: bfloat16 [128, 16, 4096], P(('section', 'expert')), may hold values from -0.125 to 0.125
- w_router: bfloat16 [16, 4096, 8], P('section', 'expert'), may hold values from -0.09375 to 0.09375
Outputs:
- grad_out: bfloat16 [2048, 4096], P('section', 'expert')
- expert_grad: bfloat16 [128, 16, 4096], P(('section', 'expert'))
The draws below stay inside these ranges and needn't reach their ends.
Inputs may be any that keep to these rules, and one draw needn't show every extreme that they name: `expert_ids`: each token names 2 different experts; within one section's micro-batch of one step (aligned blocks of 128 rows) no expert is named by more than 40 tokens, a bound that some block reaches. The gates of a token sum to one, the first the larger.
All inputs are finite; a program needn't handle non-finite values.
Results may differ from the reference program's by a relative error of at most 0.0085.
Values may be sent and summed in bfloat16 or wider, within the bound.
A program may use at most 64 MiB of HBM per device.

```python
import math
import jax
import jax.numpy as jnp
import numpy as np
from jax import lax

D = 4096
F = 16
TOP = 2
TICKS = 4
TOKENS = 128
SECTIONS = 16
SEGMENTS = 16
E = 8
CAP = 40


def draw_incoming(key, part):
    key_base, key_cols = jax.random.split(key)
    section_index = (jnp.arange(SECTIONS * TOKENS) // TOKENS).astype(jnp.float32)
    section_span = max(SECTIONS - 1, 1)
    column_scale = jnp.exp(jax.random.uniform(key_cols, (SECTIONS, 1, D), jnp.float32, math.log(0.3), math.log(3.0)))
    column_scale = jnp.broadcast_to(column_scale, (SECTIONS, TOKENS, D)).reshape(SECTIONS * TOKENS, D)
    base_draw = jnp.clip(jax.random.normal(key_base, (SECTIONS * TOKENS, D), jnp.float32), -5.0, 5.0)
    section_ramp = jnp.sqrt(1.0 + 2.0 * section_index / section_span)
    return (base_draw * column_scale * section_ramp[:, None]).astype(jnp.bfloat16)


def draw_gates(key, part):
    upper_end = 0.95
    leading = jax.random.uniform(key, (TICKS, SECTIONS * TOKENS, 1), jnp.float32, 0.5, upper_end)
    return jnp.concatenate([leading, 1.0 - leading], axis=2)


def block_levels(rng, dims, shards, least, largest):
    factor_of, own = 1.0, jax.random.fold_in(rng, 6)
    for position, parts in shards:
        heights = jnp.exp(jax.random.uniform(jax.random.fold_in(own, position), (parts,), jnp.float32, least / len(shards), largest / len(shards)))
        factor_of = factor_of * jnp.repeat(heights, dims[position] // parts).reshape([-1 if axis == position else 1 for axis in range(len(dims))])
    return factor_of


def shared_out(own_key, own, number, rows, count, top, reach, skew):
    sequence = jax.random.permutation(own_key, count)
    crowded, common = portions_of(count, rows * top, reach, skew, True), portions_of(count, rows * top, reach, skew, False)
    places = jnp.arange(count)

    def named(sizes, offset_by):
        used = int((sizes > 0).sum())
        fixed = max(1, used // 4)
        passed = fixed + (places - fixed + offset_by * (used - fixed)) % max(1, count - fixed)
        return jnp.zeros((count,), jnp.int32).at[sequence[jnp.where(places < fixed, places, passed)]].set(jnp.asarray(sizes, jnp.int32))

    sizes = jnp.where(number % 4 == 0, named(crowded, number // 4), named(common, number - number // 4 - 1))
    mixed = jax.random.permutation(jax.random.fold_in(own, 3), count)
    source_of, taker = mixed[0:count // 2 * 2:2], mixed[1:count // 2 * 2:2]
    slack = jnp.minimum(sizes[source_of] - 1, reach - sizes[taker]) // 2
    slack = jnp.where((source_of == sequence[0]) | (taker == sequence[0]) | (sizes[taker] == 0), 0, jnp.maximum(slack, 0))
    passed = jax.random.randint(jax.random.fold_in(own, 4), (count // 2,), 0, 1 << 20) % (slack + 1)
    sizes = sizes.at[source_of].add(-passed).at[taker].add(passed)
    members = jnp.searchsorted(jnp.cumsum(sizes), jnp.arange(rows * top), side="right").astype(jnp.int32)
    table = members.reshape(top, rows).T
    table = table[jax.random.permutation(jax.random.fold_in(own, 1), rows)]
    offset_by = jax.random.randint(jax.random.fold_in(own, 2), (rows, 1), 0, top)
    return jnp.take_along_axis(table, (jnp.arange(top)[None, :] + offset_by) % top, axis=1)


def portions_of(amount, total, most, slope, full):
    portions = [(1 << 20) // math.isqrt(rank ** slope) + 1 for rank in range(1, amount + 1)]
    largest = most if full else min(most, max(-(-total // amount), total * portions[0] // sum(portions)))
    least = 1 if total - largest >= amount - 1 else 0
    holding, surplus = [largest] + [least] * (amount - 1), total - largest - least * (amount - 1)
    while surplus > 0:
        candidates = [i for i in range(1, amount) if holding[i] < largest] or [i for i in range(1, amount) if holding[i] < most]
        pool, left = sum([portions[i] for i in candidates]), surplus
        for i in candidates:
            addition = min(most - holding[i], max(1, left * portions[i] // pool), surplus)
            holding[i] = holding[i] + addition
            surplus = surplus - addition
    return np.array(holding)


def noise(stream_key, extent, deviation, bound, cuts=(), kind=jnp.bfloat16):
    values = jax.random.normal(stream_key, extent, jnp.float32) * deviation
    if len(cuts) > 0:
        values = block_levels(stream_key, extent, cuts, -0.22, 0.18) * values
    return jnp.clip(values, min=-bound, max=bound).astype(kind)


def setup_inputs(seed: int = 0) -> dict:
    key_list = jax.random.split(jax.random.key(seed), 9)
    incoming = draw_incoming(jax.random.fold_in(key_list[8], 71), 0)
    expert_ids_keys = jax.random.split(jax.random.fold_in(key_list[1], 1), TICKS * (SECTIONS * TOKENS) // TOKENS)
    expert_ids_turns = jax.random.permutation(jax.random.fold_in(key_list[1], 3), TICKS * (SECTIONS * TOKENS) // TOKENS)
    expert_ids = jax.vmap(lambda own, number: shared_out(jax.random.fold_in(key_list[1], 2), own, number, TOKENS, E, TOP, CAP, 2))(expert_ids_keys, expert_ids_turns).reshape((TICKS, SECTIONS * TOKENS, TOP))
    gates = draw_gates(jax.random.fold_in(key_list[8], 71), 0)
    pre_act = noise(key_list[3], (TICKS, SECTIONS * E * CAP, F), 1.5, 8.0, ((1, 32),))
    w_up = noise(key_list[4], (SECTIONS * E, F, D), D ** -0.5, 0.09375, ((0, 32),))
    w_down = noise(key_list[5], (SECTIONS * E, F, D), F ** -0.5, 1.5, ((0, 32),))
    delta = noise(key_list[6], (SECTIONS * E, F, D), 0.02, 0.125, ((0, 32),))
    w_router = noise(key_list[7], (SECTIONS, D, E), D ** -0.5, 0.09375, ((0, 16), (1, 2)))
    return dict(incoming=incoming, expert_ids=expert_ids, gates=gates, pre_act=pre_act, w_up=w_up, w_down=w_down, delta=delta, w_router=w_router)


COMPENSATION = 0.5
CLIP_LEVEL = 1.0

def silu_grad(pre_float):
    sigmoid_val = jax.nn.sigmoid(pre_float)
    return sigmoid_val * (1.0 + pre_float * (1.0 - sigmoid_val))

def slot_places(routing, expert_count, capacity):
    flat_ids = routing.reshape(-1).astype(jnp.int32)
    onehot = (flat_ids[:, None] == jnp.arange(expert_count, dtype=jnp.int32)[None, :]).astype(jnp.int32)
    earlier = jnp.cumsum(onehot, axis=0) - onehot
    slot_index = lax.optimization_barrier(jnp.sum(earlier * onehot, axis=1)).astype(jnp.int32)
    return (flat_ids * capacity + slot_index).astype(jnp.int32)

def token_side(current, routing, gate_vals, places, row_grad, gate_grad, router_weight, expert_count):
    token_count = routing.shape[0]
    top_count = routing.shape[1]
    flat_rows = row_grad.reshape(-1, row_grad.shape[-1])
    picked = jnp.take(flat_rows, places, axis=0).reshape(token_count, top_count, -1).astype(jnp.float32)
    mixture = lax.optimization_barrier(jnp.sum(picked, axis=1))
    chosen_grad = jnp.take(gate_grad.reshape(-1), places, axis=0).reshape(token_count, top_count)
    logit_grad = gate_vals * (chosen_grad - lax.optimization_barrier(jnp.sum(gate_vals * chosen_grad, axis=1, keepdims=True)))
    onehot = (routing[:, :, None] == jnp.arange(expert_count, dtype=jnp.int32)[None, None, :]).astype(jnp.float32)
    router_in = lax.optimization_barrier(jnp.sum(logit_grad[:, :, None] * onehot, axis=1)).astype(jnp.bfloat16)
    router_term = jnp.dot(router_in, router_weight.T, preferred_element_type=jnp.float32)
    return (current.astype(jnp.float32) + mixture + router_term).astype(jnp.bfloat16)

def segment_backward(current, routing, gate_vals, pre_block, up_weight, down_weight, router_weight):
    token_count = routing.shape[0]
    top_count = routing.shape[1]
    expert_count = pre_block.shape[0]
    capacity = pre_block.shape[1]
    places = slot_places(routing, expert_count, capacity)
    owners = (jnp.arange(token_count * top_count, dtype=jnp.int32) // top_count).astype(jnp.int32)
    slot_table = jnp.full((expert_count * capacity,), token_count, jnp.int32).at[places].set(owners)
    padded = jnp.concatenate([current, jnp.zeros((1, current.shape[1]), current.dtype)], axis=0)
    routed = jnp.take(padded, slot_table, axis=0).reshape(expert_count, capacity, current.shape[1])
    gate_table = jnp.zeros((expert_count * capacity,), jnp.float32).at[places].set(gate_vals.reshape(-1)).reshape(expert_count, capacity)
    pre_float = pre_block.astype(jnp.float32)
    hidden = jax.nn.silu(pre_float).astype(jnp.bfloat16)
    expert_out = jnp.einsum('ecf,efd->ecd', hidden.astype(jnp.float32), down_weight.astype(jnp.float32))
    gate_grad = lax.optimization_barrier(jnp.sum(routed.astype(jnp.float32) * expert_out, axis=2))
    gated_rows = (gate_table[:, :, None] * routed.astype(jnp.float32)).astype(jnp.bfloat16)
    hidden_grad = jnp.einsum('ecd,efd->ecf', gated_rows.astype(jnp.float32), down_weight.astype(jnp.float32))
    act_grad = (hidden_grad * silu_grad(pre_float)).astype(jnp.bfloat16)
    row_grad = jnp.einsum('ecf,efd->ecd', act_grad.astype(jnp.float32), up_weight.astype(jnp.float32)).astype(jnp.bfloat16)
    weight_grad = jnp.einsum('ecf,ecd->efd', hidden.astype(jnp.float32), gated_rows.astype(jnp.float32))
    updated = token_side(current, routing, gate_vals, places, row_grad, gate_grad, router_weight, expert_count)
    return (updated, weight_grad)

def one_segment(pieces):
    return segment_backward(pieces[0], pieces[1], pieces[2], pieces[3], pieces[4], pieces[5], pieces[6])

def reference(incoming, expert_ids, gates, pre_act, w_up, w_down, delta, w_router):
    current = incoming.reshape(SECTIONS, TOKENS, D)
    routing = expert_ids.reshape(TICKS, SECTIONS, TOKENS, TOP)
    gate_all = gates.reshape(TICKS, SECTIONS, TOKENS, TOP)
    pre_all = pre_act.reshape(TICKS, SECTIONS, E, CAP, F)
    up_all = w_up.reshape(SECTIONS, E, F, D)
    down_all = w_down.reshape(SECTIONS, E, F, D)
    last_segment = jnp.arange(SECTIONS, dtype=jnp.int32) % SEGMENTS == SEGMENTS - 1
    accumulated = jnp.zeros((SECTIONS, E, F, D), jnp.float32)
    for moment in range(TICKS):
        updated, weight_grad = lax.map(one_segment, (current, routing[moment], gate_all[moment], pre_all[moment], up_all, down_all, w_router))
        accumulated = accumulated + weight_grad
        if moment + 1 < TICKS:
            shifted = jnp.concatenate([updated[1:], jnp.zeros((1, TOKENS, D), updated.dtype)], axis=0)
            current = jnp.where(last_segment[:, None, None], jnp.zeros_like(shifted), shifted)
        else:
            current = updated
    compensated = accumulated + COMPENSATION * accumulated * accumulated * delta.reshape(SECTIONS, E, F, D).astype(jnp.float32)
    root_mean = jnp.sqrt(jnp.sum(compensated * compensated) / compensated.size + 1e-06)
    factor = jnp.minimum(1.0, CLIP_LEVEL / root_mean)
    expert_grad = (compensated * factor).astype(jnp.bfloat16).reshape(SECTIONS * E, F, D)
    return (current.reshape(SECTIONS * TOKENS, D), expert_grad)
```

```python
import functools

import jax
import jax.numpy as jnp
from jax import lax
from jax.experimental import pallas as pl
from jax.experimental.pallas import tpu as pltpu
from jax.sharding import PartitionSpec as P

COMPENSATION = 0.5
CLIP_LEVEL = 1.0
BLOCKS = (4, 4, 4, 4)
CHUNKS = 4
PIECES = 4
RADIX = 16
F32 = jnp.float32
BF16 = jnp.bfloat16


def dot(a, b):
    return lax.dot_general(a, b, (((1,), (0,)), ((), ())), preferred_element_type=F32)


def dot_nt(a, b):
    return lax.dot_general(a, b, (((1,), (1,)), ((), ())), preferred_element_type=F32)


def ones_where(mask):
    return jnp.where(mask, 1.0, 0.0).astype(BF16)


def round_strides(sections):
    strides = []
    stride = min(RADIX, sections)
    while stride < sections:
        strides.append(stride)
        stride *= min(RADIX, sections // stride)
    return strides


def kernel(
    sections,
    capacity,
    inc,
    ids_hbm,
    gates_hbm,
    pre_hbm,
    wup,
    wdn,
    delta,
    wr_hbm,
    gout,
    acc,
    scale,
    cur,
    cur_o,
    upd,
    wd,
    wcat,
    dl,
    pre_o,
    p_own,
    p_in,
    hid,
    slope,
    gexp,
    hgt,
    mine,
    first_in,
    later_in,
    later_out,
    local_sem,
    w_send,
    w_recv,
    p_send,
    p_recv,
    o_send,
    o_recv,
    r_send,
    r_recv,
    f_send,
    f_recv,
    l_send,
    l_recv,
    entered,
    same,
    ids,
    gates,
    pre,
    wr,
):
    steps, tokens, half = cur.shape
    width = wd.shape[0]
    rows_own = wdn.shape[0]
    hidden_units = pre.shape[1]
    slots = pre.shape[2]
    own_experts = slots // capacity
    shift_bits = hidden_units.bit_length() - 1
    chunk = tokens // CHUNKS
    piece = half // PIECES
    core = lax.axis_index("expert")
    other = 1 - core
    section = lax.axis_index("section")
    is_last = section == sections - 1
    partner = {"section": section, "expert": other}
    group = min(RADIX, sections)
    strides = round_strides(sections)

    below = {"section": jnp.maximum(section - 1, 0), "expert": core}

    def group_peer(d):
        place = (section % group) * 2 + core
        place = (place + d) % (2 * group)
        return {"section": section - section % group + place // 2, "expert": place % 2}

    def later_peer(stride, d):
        size = min(RADIX, sections // stride)
        digit = (section // stride) % size
        moved = (digit + d) % size
        return {"section": section + (moved - digit) * stride, "expert": core}

    own_cols = pl.ds(pl.multiple_of(core * half, 128), half)
    other_cols = pl.ds(pl.multiple_of(other * half, 128), half)
    own_rows = pl.ds(pl.multiple_of(core * rows_own, rows_own), rows_own)

    local = [
        pltpu.make_async_copy(inc, cur.at[0], local_sem.at[0]),
        pltpu.make_async_copy(wdn.at[:, own_cols], wd.at[own_rows, :], local_sem.at[1]),
        pltpu.make_async_copy(wup.at[:, own_cols], wcat.at[own_rows, :], local_sem.at[2]),
        pltpu.make_async_copy(delta, dl, local_sem.at[3]),
        pltpu.make_async_copy(ids_hbm, ids, local_sem.at[4]),
        pltpu.make_async_copy(gates_hbm, gates, local_sem.at[5]),
        pltpu.make_async_copy(pre_hbm, pre, local_sem.at[6]),
        pltpu.make_async_copy(wr_hbm, wr, local_sem.at[7]),
    ]
    for copy in local:
        copy.start()

    above = {"section": jnp.minimum(section + 1, sections - 1), "expert": core}
    barrier = pltpu.get_barrier_semaphore()

    def signal(sem, peer):
        pl.semaphore_signal(sem, inc=1, device_id=peer, device_id_type=pl.DeviceIdType.MESH)

    signal(barrier, partner)

    @pl.when(jnp.logical_not(is_last))
    def _():
        signal(barrier, above)

    def remote(src, dst, send, recv, device):
        return pltpu.make_async_remote_copy(
            src_ref=src,
            dst_ref=dst,
            send_sem=send,
            recv_sem=recv,
            device_id=device,
            device_id_type=pl.DeviceIdType.MESH,
        )

    pl.semaphore_wait(barrier, 1 + jnp.where(section > 0, 1, 0))

    known = max(1, (sections - 1).bit_length())

    def tell(r):
        hop = 1 << r

        @pl.when(section >= hop)
        def _():
            signal(entered.at[r], {"section": jnp.maximum(section - hop, 0), "expert": core})

        @pl.when(section + hop < sections)
        def _():
            signal(entered.at[r], {"section": jnp.minimum(section + hop, sections - 1), "expert": core})

    def hear(r):
        hop = 1 << r
        heard = jnp.where(section >= hop, 1, 0) + jnp.where(section + hop < sections, 1, 0)
        pl.semaphore_wait(entered.at[r], heard)

    def learn(low, high):
        for r in range(low, min(high, known)):
            if r:
                hear(r - 1)
            tell(r)

    weights = [
        remote(wdn.at[:, other_cols], wd.at[own_rows, :], w_send.at[1], w_recv.at[1], partner),
        remote(pre_hbm, pre_o, w_send.at[0], w_recv.at[0], partner),
        remote(wup.at[:, other_cols], wcat.at[own_rows, :], w_send.at[2], w_recv.at[2], partner),
    ]
    for copy in weights:
        copy.start()

    @pl.when(is_last)
    def _():
        for k in range(1, steps):
            cur[k] = jnp.zeros((tokens, half), BF16)

    def rows_of(q, size):
        return pl.ds(pl.multiple_of(q * size, size), size)

    def p_copy(k, q):
        rows = rows_of(q, tokens // BLOCKS[k])
        return remote(p_own.at[k, rows, :], p_in.at[k, rows, :], p_send.at[k, q], p_recv.at[k, q], partner)

    def o_copy(k, q):
        rows = rows_of(q, tokens // BLOCKS[k])
        return remote(cur.at[k, rows, :], cur_o.at[k, rows, :], o_send.at[k, q], o_recv.at[k, q], partner)

    first_o = remote(inc, cur_o.at[0], o_send.at[0, 0], o_recv.at[0, 0], partner)

    def relay(k, i):
        rows = rows_of(i, chunk)
        return remote(upd.at[k, rows, :], cur.at[k + 1, rows, :], r_send.at[k, i], r_recv.at[k, i], below)

    unit_row = lax.broadcasted_iota(jnp.int32, (width, tokens), 0)
    expert = lax.shift_right_logical(unit_row, shift_bits)
    head = (unit_row & (hidden_units - 1)) == 0

    def spread(router):
        row = lax.broadcasted_iota(jnp.int32, (width, router.shape[0]), 0)
        col = lax.broadcasted_iota(jnp.int32, (width, router.shape[0]), 1)
        return dot(ones_where(row == col * hidden_units), router[...]).astype(BF16)

    def fill_constants():
        a = lax.broadcasted_iota(jnp.int32, (width, width), 0)
        b = lax.broadcasted_iota(jnp.int32, (width, width), 1)
        same[...] = ones_where(
            lax.shift_right_logical(a, shift_bits) == lax.shift_right_logical(b, shift_bits)
        )
        wcat[width:, :] = spread(wr)

    def block_diagonal(pre_block, start):
        row = lax.broadcasted_iota(jnp.int32, (width, hidden_units), 0)
        unit = lax.broadcasted_iota(jnp.int32, (width, hidden_units), 1)
        tiled = dot(ones_where((row & (hidden_units - 1)) == unit), pre_block)
        row = lax.broadcasted_iota(jnp.int32, (width, slots), 0)
        col = lax.broadcasted_iota(jnp.int32, (width, slots), 1)
        low = (lax.shift_right_logical(row, shift_bits) - start) * capacity
        return jnp.where((col >= low) & (col < low + capacity), tiled, 0.0).astype(BF16)

    def prepare(k):
        routing = ids[k]
        gate_vals = gates[k]
        id0, id1 = routing[0:1, :], routing[1:2, :]
        g0, g1 = gate_vals[0:1, :], gate_vals[1:2, :]
        on0, on1 = id0 == expert, id1 == expert
        gate = jnp.where(on0, g0, jnp.where(on1, g1, 0.0))
        row = lax.broadcasted_iota(jnp.int32, (tokens, tokens), 0)
        col = lax.broadcasted_iota(jnp.int32, (tokens, tokens), 1)
        slot = dot(ones_where(on0 | on1), ones_where(row < col))
        slot0 = jnp.sum(jnp.where(on0 & head, slot, 0.0), axis=0, keepdims=True)
        slot1 = jnp.sum(jnp.where(on1 & head, slot, 0.0), axis=0, keepdims=True)
        place0 = id0 * capacity + slot0.astype(jnp.int32)
        place1 = id1 * capacity + slot1.astype(jnp.int32)
        at = lax.broadcasted_iota(jnp.int32, (slots, tokens), 0)
        act = jnp.zeros((width, tokens), F32)
        for ref, side in ((pre, core), (pre_o, other)):
            start = side * own_experts
            here = at + start * capacity
            picked = ones_where((here == place0) | (here == place1))
            act = act + dot(block_diagonal(ref[k], start), picked)
        sig = 1.0 / (1.0 + jnp.exp(-act))
        hidden = (act * sig).astype(BF16).astype(F32)
        hgt[k // 2, :, pl.ds(k % 2 * tokens, tokens)] = (hidden * gate).astype(BF16)
        hid[k] = jnp.transpose(hidden)
        slope[k] = jnp.transpose(sig * (1.0 + act * (1.0 - sig)) * gate)
        gexp[k] = jnp.transpose(gate)

    def stage_a(k, q):
        rows = rows_of(q, tokens // BLOCKS[k])
        p_own[k, rows, :] = dot_nt(cur[k, rows, :], wd[...])
        p_copy(k, q).start()

    def coefficients(k, q):
        rows = rows_of(q, tokens // BLOCKS[k])
        p_copy(k, q).wait_recv()
        total = p_own[k, rows, :] + p_in[k, rows, :]
        hidden = hid[k, rows, :]
        gate = gexp[k, rows, :]
        product = hidden * total
        high = product.astype(BF16)
        low = (product - high.astype(F32)).astype(BF16)
        summed = same[...]
        gate_grad = dot(high, summed) + dot(low, summed)
        mean = jnp.sum(gate * product, axis=1, keepdims=True)
        logit = (gate * (gate_grad - mean)).astype(BF16)
        act = (slope[k, rows, :] * total).astype(BF16)
        both = jnp.concatenate([act, logit], axis=1)
        return both

    def advance(base, both, table, rows, put):
        for n in range(PIECES):
            cols = pl.ds(n * piece, piece)
            value = base[rows, cols].astype(F32) + dot(both, table[:, cols])
            put(cols, value.astype(BF16))

    def stage_b(k, q):
        rows = rows_of(q, tokens // BLOCKS[k])
        both = coefficients(k, q)

        def put(cols, value):
            if k == steps - 1:
                gout[rows, cols] = value
            else:
                upd[k, rows, cols] = value

        advance(cur.at[k], both, wcat, rows, put)
        if k == steps - 1:
            return
        per = CHUNKS // BLOCKS[k]

        @pl.when(section > 0)
        def _():
            for j in range(per):
                relay(k, q * per + j).start()

    def arrive(k, q):
        per = CHUNKS // BLOCKS[k]

        @pl.when(jnp.logical_not(is_last))
        def _():
            for j in range(per):
                relay(k - 1, q * per + j).wait_recv()

        o_copy(k, q).start()

    def weight_piece(pair, n, side):
        cols = pl.ds(pl.multiple_of(n * piece, 128), piece)
        ref = cur_o if side else cur
        block = ref[2 * pair : 2 * pair + 2, :, cols].reshape(2 * tokens, piece)
        return dot(hgt[pair, own_rows, :], block)

    def loop(body, count):
        def step(q, carry):
            body(q)
            return carry

        lax.fori_loop(0, count, step, 0)

    for copy in local[4:]:
        copy.wait()
    fill_constants()
    weights[1].wait_recv()
    prepare(0)
    local[0].wait()
    local[1].wait()
    weights[0].wait_recv()
    p_own[0] = dot_nt(cur[0], wd[...])
    loop(lambda q: p_copy(0, q).start(), BLOCKS[0])
    local[2].wait()
    weights[2].wait_recv()
    loop(lambda q: stage_b(0, q), BLOCKS[0])

    first_o.start()
    for k in range(1, steps):
        prepare(k)

    def early(n):
        cols = pl.ds(pl.multiple_of(n * piece, 128), piece)
        for side in (0, 1):
            acc[side, :, cols] = weight_piece(0, n, side)

    def middle(k):
        def body(q):
            arrive(k, q)
            stage_a(k, q)
            stage_b(k, q)

        return body

    loop(middle(1), BLOCKS[1])
    learn(0, 1)
    first_o.wait_recv()
    loop(lambda q: o_copy(1, q).wait_recv(), BLOCKS[1])
    loop(early, PIECES)
    learn(1, 2)
    loop(middle(2), BLOCKS[2])
    learn(2, 3)
    last = steps - 1
    final = BLOCKS[last] - 1

    loop(middle(last), final)
    local[3].wait()
    learn(3, known)
    arrive(last, final)
    squares = jnp.zeros((1, piece), F32)
    for side, here in ((0, core), (1, other)):
        if side:
            stage_a(last, final)
            for k in (last - 1, last):
                loop(lambda q: o_copy(k, q).wait_recv(), BLOCKS[k])
        for n in range(PIECES):
            cols = pl.ds(n * piece, piece)
            shift = dl[:, pl.ds(pl.multiple_of(here * half + n * piece, 128), piece)].astype(F32)
            grad = acc[side, :, cols] + weight_piece(1, n, side)
            value = grad + COMPENSATION * grad * grad * shift
            acc[side, :, cols] = value
            squares = squares + jnp.sum(value * value, axis=0, keepdims=True)
    hear(known - 1)
    mine[...] = jnp.broadcast_to(jnp.sum(squares, axis=1, keepdims=True), mine.shape)

    firsts = [
        remote(mine, first_in.at[d], f_send.at[d], f_recv.at[d], group_peer(d))
        for d in range(1, 2 * group)
    ]
    for copy in firsts:
        copy.start()
    stage_b(last, final)
    for copy in weights + [first_o]:
        copy.wait_send()

    @pl.when(section > 0)
    def _():
        for k in range(last):
            loop(lambda i: relay(k, i).wait_send(), CHUNKS)

    for k in range(steps):
        loop(lambda q: p_copy(k, q).wait_send(), BLOCKS[k])
        if k:
            loop(lambda q: o_copy(k, q).wait_send(), BLOCKS[k])

    total = mine[...]
    for d, copy in enumerate(firsts):
        copy.wait_recv()
        total = total + first_in[d + 1]
    later = []
    for r, stride in enumerate(strides):
        later_out[r] = total
        copies = [
            remote(
                later_out.at[r],
                later_in.at[r, d],
                l_send.at[r, d],
                l_recv.at[r, d],
                later_peer(stride, d),
            )
            for d in range(1, min(RADIX, sections // stride))
        ]
        for copy in copies:
            copy.start()
        for d, copy in enumerate(copies):
            copy.wait_recv()
            total = total + later_in[r, d + 1]
        later += copies
    entries = sections * 2 * rows_own * 2 * half
    root_mean = jnp.sqrt(total / entries + 1e-06)
    scale[...] = jnp.minimum(1.0, CLIP_LEVEL / root_mean)

    for copy in firsts + later:
        copy.wait_send()


def finish(updated, compensated, scale, gout, eout, scaled, sem):
    half = scaled.shape[2]
    core = lax.axis_index("expert")
    copies = [pltpu.make_async_copy(updated, gout, sem.at[0])]
    copies[0].start()
    factor = scale[0:1, 0:1]
    for side, here in ((0, core), (1, 1 - core)):
        scaled[side] = (compensated[side] * factor).astype(BF16)
        cols = pl.ds(pl.multiple_of(here * half, 128), half)
        copies.append(pltpu.make_async_copy(scaled.at[side], eout.at[:, cols], sem.at[side + 1]))
        copies[-1].start()
    for copy in copies:
        copy.wait()


def per_device(incoming, expert_ids, gates, pre_act, w_up, w_down, delta, w_router):
    sections = lax.axis_size("section")
    steps = expert_ids.shape[0]
    tokens, half = incoming.shape
    local_experts, hidden_units, features = w_up.shape
    slots = pre_act.shape[1]
    rows_own = local_experts * hidden_units
    width = 2 * rows_own
    strides = round_strides(sections)
    rounds = max(1, len(strides))
    group = min(RADIX, sections)
    flat = (rows_own, features)
    vmem = pl.BlockSpec(memory_space=pltpu.VMEM)
    hbm = pl.BlockSpec(memory_space=pltpu.HBM)
    dma = pltpu.SemaphoreType.DMA
    updated, compensated, scale = pl.pallas_call(
        functools.partial(kernel, sections, slots // local_experts),
        out_shape=(
            jax.ShapeDtypeStruct((tokens, half), BF16),
            jax.ShapeDtypeStruct((2, rows_own, half), F32),
            jax.ShapeDtypeStruct((8, 128), F32),
        ),
        in_specs=[hbm] * 8,
        out_specs=(vmem, vmem, vmem),
        scratch_shapes=[
            pltpu.VMEM((steps, tokens, half), BF16),
            pltpu.VMEM((steps, tokens, half), BF16),
            pltpu.VMEM((steps - 1, tokens, half), BF16),
            pltpu.VMEM((width, half), BF16),
            pltpu.VMEM((2 * width, half), BF16),
            pltpu.VMEM(flat, BF16),
            pltpu.VMEM((steps, hidden_units, slots), BF16),
            pltpu.VMEM((steps, tokens, width), F32),
            pltpu.VMEM((steps, tokens, width), F32),
            pltpu.VMEM((steps, tokens, width), F32),
            pltpu.VMEM((steps, tokens, width), F32),
            pltpu.VMEM((steps, tokens, width), F32),
            pltpu.VMEM((steps // 2, width, 2 * tokens), BF16),
            pltpu.VMEM((8, 128), F32),
            pltpu.VMEM((2 * group, 8, 128), F32),
            pltpu.VMEM((rounds, RADIX, 8, 128), F32),
            pltpu.VMEM((rounds, 8, 128), F32),
            dma((8,)),
            dma((3,)),
            dma((3,)),
            dma((steps, CHUNKS)),
            dma((steps, CHUNKS)),
            dma((steps, CHUNKS)),
            dma((steps, CHUNKS)),
            dma((steps - 1, CHUNKS)),
            dma((steps - 1, CHUNKS)),
            dma((2 * group,)),
            dma((2 * group,)),
            dma((rounds, RADIX)),
            dma((rounds, RADIX)),
            pltpu.SemaphoreType.REGULAR((max(1, (sections - 1).bit_length()),)),
            pltpu.VMEM((width, width), BF16),
            pltpu.VMEM((steps, 2, tokens), jnp.int32),
            pltpu.VMEM((steps, 2, tokens), F32),
            pltpu.VMEM((steps, hidden_units, slots), BF16),
            pltpu.VMEM((w_router.shape[2], half), BF16),
        ],
        compiler_params=pltpu.CompilerParams(
            collective_id=0, has_side_effects=True, vmem_limit_bytes=40 * 1024 * 1024
        ),
        name="relay",
    )(
        *[pltpu.with_memory_space_constraint(x, pltpu.HBM) for x in (
        incoming,
        expert_ids.transpose(0, 2, 1),
        gates.transpose(0, 2, 1),
        pre_act.transpose(0, 2, 1),
        w_up.reshape(flat),
        w_down.reshape(flat),
        delta.reshape(flat),
        w_router[0].T,
        )]
    )
    grad_out, expert_grad = pl.pallas_call(
        finish,
        out_shape=(
            jax.ShapeDtypeStruct((tokens, half), BF16),
            jax.ShapeDtypeStruct(flat, BF16),
        ),
        in_specs=[vmem, vmem, vmem],
        out_specs=(hbm, hbm),
        scratch_shapes=[pltpu.VMEM((2, rows_own, half), BF16), dma((3,))],
        compiler_params=pltpu.CompilerParams(vmem_limit_bytes=8 * 1024 * 1024),
        name="finish",
    )(updated, compensated, scale)
    return (grad_out, expert_grad.reshape(w_down.shape))


def solution(mesh):
    return jax.shard_map(
        per_device,
        mesh=mesh,
        in_specs=(
            P("section", "expert"),
            P(None, "section", None),
            P(None, "section", None),
            P(None, ("section", "expert"), None),
            P(("section", "expert"), None, None),
            P(("section", "expert"), None, None),
            P(("section", "expert"), None, None),
            P("section", "expert", None),
        ),
        out_specs=(P("section", "expert"), P(("section", "expert"), None, None)),
        check_vma=False,
    )
```

```python
import functools

import jax
import jax.numpy as jnp
from jax import lax
from jax.experimental import pallas as pl
from jax.experimental.pallas import tpu as pltpu
from jax.sharding import PartitionSpec as P

COMPENSATION = 0.5
CLIP_LEVEL = 1.0
BLOCKS = (4, 4, 4, 4)
CHUNKS = 4
LESSONS = ((), ((0, 0, 1), (2, 1, 2)), ((0, 2, 3), (2, 3, 4)), ((0, 4, 32),))
PIECES = 4
RADIX = 16
F32 = jnp.float32
BF16 = jnp.bfloat16


def dot(a, b):
    return lax.dot_general(a, b, (((1,), (0,)), ((), ())), preferred_element_type=F32)


def dot_nt(a, b):
    return lax.dot_general(a, b, (((1,), (1,)), ((), ())), preferred_element_type=F32)


def ones_where(mask):
    return jnp.where(mask, 1.0, 0.0).astype(BF16)


def round_strides(sections):
    strides = []
    stride = min(RADIX, sections)
    while stride < sections:
        strides.append(stride)
        stride *= min(RADIX, sections // stride)
    return strides


def kernel(
    sections,
    capacity,
    inc,
    ids_hbm,
    gates_hbm,
    pre_hbm,
    wup,
    wdn,
    delta,
    wr_hbm,
    gout,
    acc,
    scale,
    cur,
    cur_o,
    upd,
    wd,
    wcat,
    dl,
    pre_o,
    p_own,
    p_in,
    hid,
    slope,
    gexp,
    hgt,
    mine,
    first_in,
    later_in,
    later_out,
    local_sem,
    w_send,
    w_recv,
    p_send,
    p_recv,
    o_send,
    o_recv,
    r_send,
    r_recv,
    f_send,
    f_recv,
    l_send,
    l_recv,
    entered,
    same,
    ids,
    gates,
    pre,
    wr,
):
    steps, tokens, half = cur.shape
    width = wd.shape[0]
    rows_own = wdn.shape[0]
    hidden_units = pre.shape[1]
    slots = pre.shape[2]
    own_experts = slots // capacity
    shift_bits = hidden_units.bit_length() - 1
    chunk = tokens // CHUNKS
    piece = half // PIECES
    core = lax.axis_index("expert")
    other = 1 - core
    section = lax.axis_index("section")
    is_last = section == sections - 1
    partner = {"section": section, "expert": other}
    group = min(RADIX, sections)
    strides = round_strides(sections)

    below = {"section": jnp.maximum(section - 1, 0), "expert": core}

    def group_peer(d):
        place = (section % group) * 2 + core
        place = (place + d) % (2 * group)
        return {"section": section - section % group + place // 2, "expert": place % 2}

    def later_peer(stride, d):
        size = min(RADIX, sections // stride)
        digit = (section // stride) % size
        moved = (digit + d) % size
        return {"section": section + (moved - digit) * stride, "expert": core}

    own_cols = pl.ds(pl.multiple_of(core * half, 128), half)
    other_cols = pl.ds(pl.multiple_of(other * half, 128), half)
    own_rows = pl.ds(pl.multiple_of(core * rows_own, rows_own), rows_own)

    local = [
        pltpu.make_async_copy(inc, cur.at[0], local_sem.at[0]),
        pltpu.make_async_copy(wdn.at[:, own_cols], wd.at[own_rows, :], local_sem.at[1]),
        pltpu.make_async_copy(wup.at[:, own_cols], wcat.at[own_rows, :], local_sem.at[2]),
        pltpu.make_async_copy(delta, dl, local_sem.at[3]),
        pltpu.make_async_copy(ids_hbm, ids, local_sem.at[4]),
        pltpu.make_async_copy(gates_hbm, gates, local_sem.at[5]),
        pltpu.make_async_copy(pre_hbm, pre, local_sem.at[6]),
        pltpu.make_async_copy(wr_hbm, wr, local_sem.at[7]),
    ]
    for copy in local:
        copy.start()

    above = {"section": jnp.minimum(section + 1, sections - 1), "expert": core}
    barrier = pltpu.get_barrier_semaphore()

    def signal(sem, peer):
        pl.semaphore_signal(sem, inc=1, device_id=peer, device_id_type=pl.DeviceIdType.MESH)

    signal(barrier, partner)

    @pl.when(jnp.logical_not(is_last))
    def _():
        signal(barrier, above)

    def remote(src, dst, send, recv, device):
        return pltpu.make_async_remote_copy(
            src_ref=src,
            dst_ref=dst,
            send_sem=send,
            recv_sem=recv,
            device_id=device,
            device_id_type=pl.DeviceIdType.MESH,
        )

    pl.semaphore_wait(barrier, 1 + jnp.where(section > 0, 1, 0))

    known = max(1, (sections - 1).bit_length())

    def tell(r):
        hop = 1 << r

        @pl.when(section >= hop)
        def _():
            signal(entered.at[r], {"section": jnp.maximum(section - hop, 0), "expert": core})

        @pl.when(section + hop < sections)
        def _():
            signal(entered.at[r], {"section": jnp.minimum(section + hop, sections - 1), "expert": core})

    def hear(r):
        hop = 1 << r
        heard = jnp.where(section >= hop, 1, 0) + jnp.where(section + hop < sections, 1, 0)
        pl.semaphore_wait(entered.at[r], heard)

    def learn(low, high):
        for r in range(low, min(high, known)):
            if r:
                hear(r - 1)
            tell(r)

    weights = [
        remote(wdn.at[:, other_cols], wd.at[own_rows, :], w_send.at[1], w_recv.at[1], partner),
        remote(pre_hbm, pre_o, w_send.at[0], w_recv.at[0], partner),
        remote(wup.at[:, other_cols], wcat.at[own_rows, :], w_send.at[2], w_recv.at[2], partner),
    ]
    for copy in weights:
        copy.start()

    for k in range(1, steps):

        @pl.when(section + k >= sections)
        def _():
            cur[k] = jnp.zeros((tokens, half), BF16)

    def rows_of(q, size):
        return pl.ds(pl.multiple_of(q * size, size), size)

    def p_copy(k, q):
        rows = rows_of(q, tokens // BLOCKS[k])
        return remote(p_own.at[k, rows, :], p_in.at[k, rows, :], p_send.at[k, q], p_recv.at[k, q], partner)

    def o_copy(k, q):
        rows = rows_of(q, tokens // BLOCKS[k])
        return remote(cur.at[k, rows, :], cur_o.at[k, rows, :], o_send.at[k, q], o_recv.at[k, q], partner)

    first_o = remote(inc, cur_o.at[0], o_send.at[0, 0], o_recv.at[0, 0], partner)

    def relay(k, i):
        rows = rows_of(i, chunk)
        return remote(upd.at[k, rows, :], cur.at[k + 1, rows, :], r_send.at[k, i], r_recv.at[k, i], below)

    unit_row = lax.broadcasted_iota(jnp.int32, (width, tokens), 0)
    expert = lax.shift_right_logical(unit_row, shift_bits)
    head = (unit_row & (hidden_units - 1)) == 0

    def spread(router):
        row = lax.broadcasted_iota(jnp.int32, (width, router.shape[0]), 0)
        col = lax.broadcasted_iota(jnp.int32, (width, router.shape[0]), 1)
        return dot(ones_where(row == col * hidden_units), router[...]).astype(BF16)

    def fill_constants():
        a = lax.broadcasted_iota(jnp.int32, (width, width), 0)
        b = lax.broadcasted_iota(jnp.int32, (width, width), 1)
        same[...] = ones_where(
            lax.shift_right_logical(a, shift_bits) == lax.shift_right_logical(b, shift_bits)
        )
        wcat[width:, :] = spread(wr)

    def block_diagonal(pre_block, start):
        row = lax.broadcasted_iota(jnp.int32, (width, hidden_units), 0)
        unit = lax.broadcasted_iota(jnp.int32, (width, hidden_units), 1)
        tiled = dot(ones_where((row & (hidden_units - 1)) == unit), pre_block)
        row = lax.broadcasted_iota(jnp.int32, (width, slots), 0)
        col = lax.broadcasted_iota(jnp.int32, (width, slots), 1)
        low = (lax.shift_right_logical(row, shift_bits) - start) * capacity
        return jnp.where((col >= low) & (col < low + capacity), tiled, 0.0).astype(BF16)

    def prepare(k):
        routing = ids[k]
        gate_vals = gates[k]
        id0, id1 = routing[0:1, :], routing[1:2, :]
        g0, g1 = gate_vals[0:1, :], gate_vals[1:2, :]
        on0, on1 = id0 == expert, id1 == expert
        gate = jnp.where(on0, g0, jnp.where(on1, g1, 0.0))
        row = lax.broadcasted_iota(jnp.int32, (tokens, tokens), 0)
        col = lax.broadcasted_iota(jnp.int32, (tokens, tokens), 1)
        slot = dot(ones_where(on0 | on1), ones_where(row < col))
        slot0 = jnp.sum(jnp.where(on0 & head, slot, 0.0), axis=0, keepdims=True)
        slot1 = jnp.sum(jnp.where(on1 & head, slot, 0.0), axis=0, keepdims=True)
        place0 = id0 * capacity + slot0.astype(jnp.int32)
        place1 = id1 * capacity + slot1.astype(jnp.int32)
        at = lax.broadcasted_iota(jnp.int32, (slots, tokens), 0)
        act = jnp.zeros((width, tokens), F32)
        for ref, side in ((pre, core), (pre_o, other)):
            start = side * own_experts
            here = at + start * capacity
            picked = ones_where((here == place0) | (here == place1))
            act = act + dot(block_diagonal(ref[k], start), picked)
        sig = 1.0 / (1.0 + jnp.exp(-act))
        hidden = (act * sig).astype(BF16).astype(F32)
        hgt[k // 2, :, pl.ds(k % 2 * tokens, tokens)] = (hidden * gate).astype(BF16)
        hid[k] = jnp.transpose(hidden)
        slope[k] = jnp.transpose(sig * (1.0 + act * (1.0 - sig)) * gate)
        gexp[k] = jnp.transpose(gate)

    def stage_a(k, q):
        rows = rows_of(q, tokens // BLOCKS[k])
        p_own[k, rows, :] = dot_nt(cur[k, rows, :], wd[...])
        p_copy(k, q).start()

    def coefficients(k, q):
        rows = rows_of(q, tokens // BLOCKS[k])
        p_copy(k, q).wait_recv()
        total = p_own[k, rows, :] + p_in[k, rows, :]
        hidden = hid[k, rows, :]
        gate = gexp[k, rows, :]
        product = hidden * total
        high = product.astype(BF16)
        low = (product - high.astype(F32)).astype(BF16)
        summed = same[...]
        gate_grad = dot(high, summed) + dot(low, summed)
        mean = jnp.sum(gate * product, axis=1, keepdims=True)
        logit = (gate * (gate_grad - mean)).astype(BF16)
        act = (slope[k, rows, :] * total).astype(BF16)
        both = jnp.concatenate([act, logit], axis=1)
        return both

    def advance(base, both, table, rows, put):
        for n in range(PIECES):
            cols = pl.ds(n * piece, piece)
            value = base[rows, cols].astype(F32) + dot(both, table[:, cols])
            put(cols, value.astype(BF16))

    def stage_b(k, q):
        rows = rows_of(q, tokens // BLOCKS[k])
        both = coefficients(k, q)

        def put(cols, value):
            if k == steps - 1:
                gout[rows, cols] = value
            else:
                upd[k, rows, cols] = value

        advance(cur.at[k], both, wcat, rows, put)
        if k == steps - 1:
            return
        per = CHUNKS // BLOCKS[k]

        @pl.when((section > 0) & (section + k < sections))
        def _():
            for j in range(per):
                relay(k, q * per + j).start()

    def arrive(k, q):
        per = CHUNKS // BLOCKS[k]

        @pl.when(section + k < sections)
        def _():
            for j in range(per):
                relay(k - 1, q * per + j).wait_recv()

        o_copy(k, q).start()

    def weight_piece(pair, n, side):
        cols = pl.ds(pl.multiple_of(n * piece, 128), piece)
        ref = cur_o if side else cur
        block = ref[2 * pair : 2 * pair + 2, :, cols].reshape(2 * tokens, piece)
        return dot(hgt[pair, own_rows, :], block)

    def loop(body, count):
        def step(q, carry):
            body(q)
            return carry

        lax.fori_loop(0, count, step, 0)

    for copy in local[4:]:
        copy.wait()
    fill_constants()
    weights[1].wait_recv()
    prepare(0)
    local[0].wait()
    local[1].wait()
    weights[0].wait_recv()
    p_own[0] = dot_nt(cur[0], wd[...])
    loop(lambda q: p_copy(0, q).start(), BLOCKS[0])
    local[2].wait()
    weights[2].wait_recv()
    loop(lambda q: stage_b(0, q), BLOCKS[0])

    first_o.start()
    for k in range(1, steps):
        prepare(k)

    def early(n):
        cols = pl.ds(pl.multiple_of(n * piece, 128), piece)
        for side in (0, 1):
            acc[side, :, cols] = weight_piece(0, n, side)

    def middle(k):
        def body(q):
            arrive(k, q)
            stage_a(k, q)
            stage_b(k, q)
            for at, low, high in LESSONS[k]:

                @pl.when(q == at)
                def _():
                    learn(low, high)

        return body

    loop(middle(1), BLOCKS[1])
    first_o.wait_recv()
    loop(lambda q: o_copy(1, q).wait_recv(), BLOCKS[1])
    loop(early, PIECES)
    loop(middle(2), BLOCKS[2])
    last = steps - 1
    final = BLOCKS[last] - 1

    loop(middle(last), final)
    local[3].wait()
    arrive(last, final)
    squares = jnp.zeros((1, piece), F32)
    for side, here in ((0, core), (1, other)):
        if side:
            stage_a(last, final)
            for k in (last - 1, last):
                loop(lambda q: o_copy(k, q).wait_recv(), BLOCKS[k])
        for n in range(PIECES):
            cols = pl.ds(n * piece, piece)
            shift = dl[:, pl.ds(pl.multiple_of(here * half + n * piece, 128), piece)].astype(F32)
            grad = acc[side, :, cols] + weight_piece(1, n, side)
            value = grad + COMPENSATION * grad * grad * shift
            acc[side, :, cols] = value
            squares = squares + jnp.sum(value * value, axis=0, keepdims=True)
    hear(known - 1)
    mine[...] = jnp.broadcast_to(jnp.sum(squares, axis=1, keepdims=True), mine.shape)

    firsts = [
        remote(mine, first_in.at[d], f_send.at[d], f_recv.at[d], group_peer(d))
        for d in range(1, 2 * group)
    ]
    for copy in firsts:
        copy.start()
    stage_b(last, final)
    for copy in weights + [first_o]:
        copy.wait_send()

    for k in range(last):

        @pl.when((section > 0) & (section + k < sections))
        def _():
            loop(lambda i: relay(k, i).wait_send(), CHUNKS)

    for k in range(steps):
        loop(lambda q: p_copy(k, q).wait_send(), BLOCKS[k])
        if k:
            loop(lambda q: o_copy(k, q).wait_send(), BLOCKS[k])

    total = mine[...]
    for d, copy in enumerate(firsts):
        copy.wait_recv()
        total = total + first_in[d + 1]
    later = []
    for r, stride in enumerate(strides):
        later_out[r] = total
        copies = [
            remote(
                later_out.at[r],
                later_in.at[r, d],
                l_send.at[r, d],
                l_recv.at[r, d],
                later_peer(stride, d),
            )
            for d in range(1, min(RADIX, sections // stride))
        ]
        for copy in copies:
            copy.start()
        for d, copy in enumerate(copies):
            copy.wait_recv()
            total = total + later_in[r, d + 1]
        later += copies
    entries = sections * 2 * rows_own * 2 * half
    root_mean = jnp.sqrt(total / entries + 1e-06)
    scale[...] = jnp.broadcast_to(jnp.minimum(1.0, CLIP_LEVEL / root_mean), scale.shape)

    for copy in firsts + later:
        copy.wait_send()


def finish(updated, compensated, scale, gout, eout, scaled, sem):
    half = scaled.shape[2]
    core = lax.axis_index("expert")
    copies = [pltpu.make_async_copy(updated, gout, sem.at[0])]
    copies[0].start()
    factor = scale[0:1, 0:1]
    for side, here in ((0, core), (1, 1 - core)):
        scaled[side] = (compensated[side] * factor).astype(BF16)
        cols = pl.ds(pl.multiple_of(here * half, 128), half)
        copies.append(pltpu.make_async_copy(scaled.at[side], eout.at[:, cols], sem.at[side + 1]))
        copies[-1].start()
    for copy in copies:
        copy.wait()


def per_device(incoming, expert_ids, gates, pre_act, w_up, w_down, delta, w_router):
    sections = lax.axis_size("section")
    steps = expert_ids.shape[0]
    tokens, half = incoming.shape
    local_experts, hidden_units, features = w_up.shape
    slots = pre_act.shape[1]
    rows_own = local_experts * hidden_units
    width = 2 * rows_own
    strides = round_strides(sections)
    rounds = max(1, len(strides))
    group = min(RADIX, sections)
    flat = (rows_own, features)
    vmem = pl.BlockSpec(memory_space=pltpu.VMEM)
    hbm = pl.BlockSpec(memory_space=pltpu.HBM)
    dma = pltpu.SemaphoreType.DMA
    updated, compensated, scale = pl.pallas_call(
        functools.partial(kernel, sections, slots // local_experts),
        out_shape=(
            jax.ShapeDtypeStruct((tokens, half), BF16),
            jax.ShapeDtypeStruct((2, rows_own, half), F32),
            jax.ShapeDtypeStruct((8, 128), F32),
        ),
        in_specs=[hbm] * 8,
        out_specs=(vmem, vmem, vmem),
        scratch_shapes=[
            pltpu.VMEM((steps, tokens, half), BF16),
            pltpu.VMEM((steps, tokens, half), BF16),
            pltpu.VMEM((steps - 1, tokens, half), BF16),
            pltpu.VMEM((width, half), BF16),
            pltpu.VMEM((2 * width, half), BF16),
            pltpu.VMEM(flat, BF16),
            pltpu.VMEM((steps, hidden_units, slots), BF16),
            pltpu.VMEM((steps, tokens, width), F32),
            pltpu.VMEM((steps, tokens, width), F32),
            pltpu.VMEM((steps, tokens, width), F32),
            pltpu.VMEM((steps, tokens, width), F32),
            pltpu.VMEM((steps, tokens, width), F32),
            pltpu.VMEM((steps // 2, width, 2 * tokens), BF16),
            pltpu.VMEM((1, 128), F32),
            pltpu.VMEM((2 * group, 1, 128), F32),
            pltpu.VMEM((rounds, RADIX, 1, 128), F32),
            pltpu.VMEM((rounds, 1, 128), F32),
            dma((8,)),
            dma((3,)),
            dma((3,)),
            dma((steps, CHUNKS)),
            dma((steps, CHUNKS)),
            dma((steps, CHUNKS)),
            dma((steps, CHUNKS)),
            dma((steps - 1, CHUNKS)),
            dma((steps - 1, CHUNKS)),
            dma((2 * group,)),
            dma((2 * group,)),
            dma((rounds, RADIX)),
            dma((rounds, RADIX)),
            pltpu.SemaphoreType.REGULAR((max(1, (sections - 1).bit_length()),)),
            pltpu.VMEM((width, width), BF16),
            pltpu.VMEM((steps, 2, tokens), jnp.int32),
            pltpu.VMEM((steps, 2, tokens), F32),
            pltpu.VMEM((steps, hidden_units, slots), BF16),
            pltpu.VMEM((w_router.shape[2], half), BF16),
        ],
        compiler_params=pltpu.CompilerParams(
            collective_id=0, has_side_effects=True, vmem_limit_bytes=40 * 1024 * 1024
        ),
        name="relay",
    )(
        *[pltpu.with_memory_space_constraint(x, pltpu.HBM) for x in (
        incoming,
        expert_ids.transpose(0, 2, 1),
        gates.transpose(0, 2, 1),
        pre_act.transpose(0, 2, 1),
        w_up.reshape(flat),
        w_down.reshape(flat),
        delta.reshape(flat),
        w_router[0].T,
        )]
    )
    grad_out, expert_grad = pl.pallas_call(
        finish,
        out_shape=(
            jax.ShapeDtypeStruct((tokens, half), BF16),
            jax.ShapeDtypeStruct(flat, BF16),
        ),
        in_specs=[vmem, vmem, vmem],
        out_specs=(hbm, hbm),
        scratch_shapes=[pltpu.VMEM((2, rows_own, half), BF16), dma((3,))],
        compiler_params=pltpu.CompilerParams(vmem_limit_bytes=8 * 1024 * 1024),
        name="finish",
    )(updated, compensated, scale)
    return (grad_out, expert_grad.reshape(w_down.shape))


def solution(mesh):
    return jax.shard_map(
        per_device,
        mesh=mesh,
        in_specs=(
            P("section", "expert"),
            P(None, "section", None),
            P(None, "section", None),
            P(None, ("section", "expert"), None),
            P(("section", "expert"), None, None),
            P(("section", "expert"), None, None),
            P(("section", "expert"), None, None),
            P("section", "expert", None),
        ),
        out_specs=(P("section", "expert"), P(("section", "expert"), None, None)),
        check_vma=False,
    )
```

```python
import functools

import jax
import jax.numpy as jnp
from jax import lax
from jax.experimental import pallas as pl
from jax.experimental.pallas import tpu as pltpu
from jax.sharding import PartitionSpec as P

COMPENSATION = 0.5
CLIP_LEVEL = 1.0
BLOCKS = (4, 4, 4, 4)
CHUNKS = 4
LESSONS = ((), ((0, 0, 1), (2, 1, 2)), ((0, 2, 3), (2, 3, 4)), ((0, 4, 32),))
PIECES = 4
RADIX = 16
F32 = jnp.float32
BF16 = jnp.bfloat16


def dot(a, b):
    return lax.dot_general(a, b, (((1,), (0,)), ((), ())), preferred_element_type=F32)


def dot_nt(a, b):
    return lax.dot_general(a, b, (((1,), (1,)), ((), ())), preferred_element_type=F32)


def ones_where(mask):
    return jnp.where(mask, 1.0, 0.0).astype(BF16)


def round_strides(sections):
    strides = []
    stride = min(RADIX, sections)
    while stride < sections:
        strides.append(stride)
        stride *= min(RADIX, sections // stride)
    return strides


def kernel(
    sections,
    capacity,
    inc,
    ids_hbm,
    gates_hbm,
    pre_hbm,
    wup,
    wdn,
    delta,
    wr_hbm,
    gout,
    acc,
    scale,
    cur,
    cur_o,
    upd,
    wd,
    wcat,
    dl,
    pre_o,
    p_own,
    p_in,
    hid,
    slope,
    gexp,
    hgt,
    mine,
    first_in,
    later_in,
    later_out,
    local_sem,
    w_send,
    w_recv,
    p_send,
    p_recv,
    o_send,
    o_recv,
    r_send,
    r_recv,
    f_send,
    f_recv,
    l_send,
    l_recv,
    entered,
    same,
    ids,
    gates,
    pre,
    wr,
):
    steps, tokens, half = cur.shape
    width = wd.shape[0]
    rows_own = wdn.shape[0]
    hidden_units = pre.shape[1]
    slots = pre.shape[2]
    own_experts = slots // capacity
    shift_bits = hidden_units.bit_length() - 1
    chunk = tokens // CHUNKS
    piece = half // PIECES
    core = lax.axis_index("expert")
    other = 1 - core
    section = lax.axis_index("section")
    is_last = section == sections - 1
    partner = {"section": section, "expert": other}
    group = min(RADIX, sections)
    strides = round_strides(sections)

    below = {"section": jnp.maximum(section - 1, 0), "expert": core}

    def group_peer(d):
        place = (section % group) * 2 + core
        place = (place + d) % (2 * group)
        return {"section": section - section % group + place // 2, "expert": place % 2}

    def later_peer(stride, d):
        size = min(RADIX, sections // stride)
        digit = (section // stride) % size
        moved = (digit + d) % size
        return {"section": section + (moved - digit) * stride, "expert": core}

    own_cols = pl.ds(pl.multiple_of(core * half, 128), half)
    other_cols = pl.ds(pl.multiple_of(other * half, 128), half)
    own_rows = pl.ds(pl.multiple_of(core * rows_own, rows_own), rows_own)

    above = {"section": jnp.minimum(section + 1, sections - 1), "expert": core}
    barrier = pltpu.get_barrier_semaphore()

    def signal(sem, peer):
        pl.semaphore_signal(sem, inc=1, device_id=peer, device_id_type=pl.DeviceIdType.MESH)

    signal(barrier, partner)

    @pl.when(jnp.logical_not(is_last))
    def _():
        signal(barrier, above)

    local = [
        pltpu.make_async_copy(inc, cur.at[0], local_sem.at[0]),
        pltpu.make_async_copy(wdn.at[:, own_cols], wd.at[own_rows, :], local_sem.at[1]),
        pltpu.make_async_copy(wup.at[:, own_cols], wcat.at[own_rows, :], local_sem.at[2]),
        pltpu.make_async_copy(delta, dl, local_sem.at[3]),
        pltpu.make_async_copy(ids_hbm, ids, local_sem.at[4]),
        pltpu.make_async_copy(gates_hbm, gates, local_sem.at[5]),
        pltpu.make_async_copy(pre_hbm, pre, local_sem.at[6]),
        pltpu.make_async_copy(wr_hbm, wr, local_sem.at[7]),
    ]
    for copy in local:
        copy.start()

    def remote(src, dst, send, recv, device):
        return pltpu.make_async_remote_copy(
            src_ref=src,
            dst_ref=dst,
            send_sem=send,
            recv_sem=recv,
            device_id=device,
            device_id_type=pl.DeviceIdType.MESH,
        )

    pl.semaphore_wait(barrier, 1 + jnp.where(section > 0, 1, 0))

    known = max(1, (sections - 1).bit_length())

    def tell(r):
        hop = 1 << r

        @pl.when(section >= hop)
        def _():
            signal(entered.at[r], {"section": jnp.maximum(section - hop, 0), "expert": core})

        @pl.when(section + hop < sections)
        def _():
            signal(entered.at[r], {"section": jnp.minimum(section + hop, sections - 1), "expert": core})

    def hear(r):
        hop = 1 << r
        heard = jnp.where(section >= hop, 1, 0) + jnp.where(section + hop < sections, 1, 0)
        pl.semaphore_wait(entered.at[r], heard)

    def learn(low, high):
        for r in range(low, min(high, known)):
            if r:
                hear(r - 1)
            tell(r)

    weights = [
        remote(wdn.at[:, other_cols], wd.at[own_rows, :], w_send.at[1], w_recv.at[1], partner),
        remote(pre_hbm, pre_o, w_send.at[0], w_recv.at[0], partner),
        remote(wup.at[:, other_cols], wcat.at[own_rows, :], w_send.at[2], w_recv.at[2], partner),
    ]
    for copy in weights:
        copy.start()

    for k in range(1, steps):

        @pl.when(section + k >= sections)
        def _():
            cur[k] = jnp.zeros((tokens, half), BF16)

    def rows_of(q, size):
        return pl.ds(pl.multiple_of(q * size, size), size)

    def p_copy(k, q):
        rows = rows_of(q, tokens // BLOCKS[k])
        return remote(p_own.at[k, rows, :], p_in.at[k, rows, :], p_send.at[k, q], p_recv.at[k, q], partner)

    def o_copy(k, q):
        rows = rows_of(q, tokens // BLOCKS[k])
        return remote(cur.at[k, rows, :], cur_o.at[k, rows, :], o_send.at[k, q], o_recv.at[k, q], partner)

    first_o = remote(inc, cur_o.at[0], o_send.at[0, 0], o_recv.at[0, 0], partner)

    def relay(k, i):
        rows = rows_of(i, chunk)
        return remote(upd.at[k, rows, :], cur.at[k + 1, rows, :], r_send.at[k, i], r_recv.at[k, i], below)

    unit_row = lax.broadcasted_iota(jnp.int32, (width, tokens), 0)
    expert = lax.shift_right_logical(unit_row, shift_bits)
    head = (unit_row & (hidden_units - 1)) == 0

    def spread(router):
        row = lax.broadcasted_iota(jnp.int32, (width, router.shape[0]), 0)
        col = lax.broadcasted_iota(jnp.int32, (width, router.shape[0]), 1)
        return dot(ones_where(row == col * hidden_units), router[...]).astype(BF16)

    def fill_constants():
        a = lax.broadcasted_iota(jnp.int32, (width, width), 0)
        b = lax.broadcasted_iota(jnp.int32, (width, width), 1)
        same[...] = ones_where(
            lax.shift_right_logical(a, shift_bits) == lax.shift_right_logical(b, shift_bits)
        )
        wcat[width:, :] = spread(wr)

    def block_diagonal(pre_block, start):
        row = lax.broadcasted_iota(jnp.int32, (width, hidden_units), 0)
        unit = lax.broadcasted_iota(jnp.int32, (width, hidden_units), 1)
        tiled = dot(ones_where((row & (hidden_units - 1)) == unit), pre_block)
        row = lax.broadcasted_iota(jnp.int32, (width, slots), 0)
        col = lax.broadcasted_iota(jnp.int32, (width, slots), 1)
        low = (lax.shift_right_logical(row, shift_bits) - start) * capacity
        return jnp.where((col >= low) & (col < low + capacity), tiled, 0.0).astype(BF16)

    def prepare(k):
        routing = ids[k]
        gate_vals = gates[k]
        id0, id1 = routing[0:1, :], routing[1:2, :]
        g0, g1 = gate_vals[0:1, :], gate_vals[1:2, :]
        on0, on1 = id0 == expert, id1 == expert
        gate = jnp.where(on0, g0, jnp.where(on1, g1, 0.0))
        row = lax.broadcasted_iota(jnp.int32, (tokens, tokens), 0)
        col = lax.broadcasted_iota(jnp.int32, (tokens, tokens), 1)
        slot = dot(ones_where(on0 | on1), ones_where(row < col))
        slot0 = jnp.sum(jnp.where(on0 & head, slot, 0.0), axis=0, keepdims=True)
        slot1 = jnp.sum(jnp.where(on1 & head, slot, 0.0), axis=0, keepdims=True)
        place0 = id0 * capacity + slot0.astype(jnp.int32)
        place1 = id1 * capacity + slot1.astype(jnp.int32)
        at = lax.broadcasted_iota(jnp.int32, (slots, tokens), 0)
        act = jnp.zeros((width, tokens), F32)
        for ref, side in ((pre, core), (pre_o, other)):
            start = side * own_experts
            here = at + start * capacity
            picked = ones_where((here == place0) | (here == place1))
            act = act + dot(block_diagonal(ref[k], start), picked)
        sig = 1.0 / (1.0 + jnp.exp(-act))
        hidden = (act * sig).astype(BF16).astype(F32)
        hgt[k // 2, :, pl.ds(k % 2 * tokens, tokens)] = (hidden * gate).astype(BF16)
        hid[k] = jnp.transpose(hidden)
        slope[k] = jnp.transpose(sig * (1.0 + act * (1.0 - sig)) * gate)
        gexp[k] = jnp.transpose(gate)

    def stage_a(k, q):
        rows = rows_of(q, tokens // BLOCKS[k])
        p_own[k, rows, :] = dot_nt(cur[k, rows, :], wd[...])
        p_copy(k, q).start()

    def coefficients(k, q):
        rows = rows_of(q, tokens // BLOCKS[k])
        p_copy(k, q).wait_recv()
        total = p_own[k, rows, :] + p_in[k, rows, :]
        hidden = hid[k, rows, :]
        gate = gexp[k, rows, :]
        product = hidden * total
        high = product.astype(BF16)
        low = (product - high.astype(F32)).astype(BF16)
        summed = same[...]
        gate_grad = dot(high, summed) + dot(low, summed)
        mean = jnp.sum(gate * product, axis=1, keepdims=True)
        logit = (gate * (gate_grad - mean)).astype(BF16)
        act = (slope[k, rows, :] * total).astype(BF16)
        both = jnp.concatenate([act, logit], axis=1)
        return both

    def advance(base, both, table, rows, put):
        for n in range(PIECES):
            cols = pl.ds(n * piece, piece)
            value = base[rows, cols].astype(F32) + dot(both, table[:, cols])
            put(cols, value.astype(BF16))

    def stage_b(k, q):
        rows = rows_of(q, tokens // BLOCKS[k])
        both = coefficients(k, q)

        def put(cols, value):
            if k == steps - 1:
                gout[rows, cols] = value
            else:
                upd[k, rows, cols] = value

        advance(cur.at[k], both, wcat, rows, put)
        if k == steps - 1:
            return
        per = CHUNKS // BLOCKS[k]

        @pl.when((section > 0) & (section + k < sections))
        def _():
            for j in range(per):
                relay(k, q * per + j).start()

    def arrive(k, q):
        per = CHUNKS // BLOCKS[k]

        @pl.when(section + k < sections)
        def _():
            for j in range(per):
                relay(k - 1, q * per + j).wait_recv()

        o_copy(k, q).start()

    def weight_piece(pair, n, side):
        cols = pl.ds(pl.multiple_of(n * piece, 128), piece)
        ref = cur_o if side else cur
        block = ref[2 * pair : 2 * pair + 2, :, cols].reshape(2 * tokens, piece)
        return dot(hgt[pair, own_rows, :], block)

    def loop(body, count):
        def step(q, carry):
            body(q)
            return carry

        lax.fori_loop(0, count, step, 0)

    for copy in local[4:]:
        copy.wait()
    fill_constants()
    local[0].wait()
    local[1].wait()
    weights[0].wait_recv()
    p_own[0] = dot_nt(cur[0], wd[...])
    loop(lambda q: p_copy(0, q).start(), BLOCKS[0])
    weights[1].wait_recv()
    prepare(0)
    local[2].wait()
    weights[2].wait_recv()
    loop(lambda q: stage_b(0, q), BLOCKS[0])

    first_o.start()
    for k in range(1, steps):
        prepare(k)

    def early(n):
        cols = pl.ds(pl.multiple_of(n * piece, 128), piece)
        for side in (0, 1):
            acc[side, :, cols] = weight_piece(0, n, side)

    def middle(k):
        def body(q):
            arrive(k, q)
            stage_a(k, q)
            stage_b(k, q)
            for at, low, high in LESSONS[k]:

                @pl.when(q == at)
                def _():
                    learn(low, high)

        return body

    loop(middle(1), BLOCKS[1])
    first_o.wait_recv()
    loop(lambda q: o_copy(1, q).wait_recv(), BLOCKS[1])
    loop(early, PIECES)
    loop(middle(2), BLOCKS[2])
    last = steps - 1
    final = BLOCKS[last] - 1

    loop(middle(last), final)
    local[3].wait()
    arrive(last, final)
    squares = jnp.zeros((1, piece), F32)
    for side, here in ((0, core), (1, other)):
        if side:
            stage_a(last, final)
            for k in (last - 1, last):
                loop(lambda q: o_copy(k, q).wait_recv(), BLOCKS[k])
        for n in range(PIECES):
            cols = pl.ds(n * piece, piece)
            shift = dl[:, pl.ds(pl.multiple_of(here * half + n * piece, 128), piece)].astype(F32)
            grad = acc[side, :, cols] + weight_piece(1, n, side)
            value = grad + COMPENSATION * grad * grad * shift
            acc[side, :, cols] = value
            squares = squares + jnp.sum(value * value, axis=0, keepdims=True)
    hear(known - 1)
    mine[...] = jnp.broadcast_to(jnp.sum(squares, axis=1, keepdims=True), mine.shape)

    firsts = [
        remote(mine, first_in.at[d], f_send.at[d], f_recv.at[d], group_peer(d))
        for d in range(1, 2 * group)
    ]
    for copy in firsts:
        copy.start()
    stage_b(last, final)
    for copy in weights + [first_o]:
        copy.wait_send()

    for k in range(last):

        @pl.when((section > 0) & (section + k < sections))
        def _():
            loop(lambda i: relay(k, i).wait_send(), CHUNKS)

    for k in range(steps):
        loop(lambda q: p_copy(k, q).wait_send(), BLOCKS[k])
        if k:
            loop(lambda q: o_copy(k, q).wait_send(), BLOCKS[k])

    total = mine[...]
    for d, copy in enumerate(firsts):
        copy.wait_recv()
        total = total + first_in[d + 1]
    later = []
    for r, stride in enumerate(strides):
        later_out[r] = total
        copies = [
            remote(
                later_out.at[r],
                later_in.at[r, d],
                l_send.at[r, d],
                l_recv.at[r, d],
                later_peer(stride, d),
            )
            for d in range(1, min(RADIX, sections // stride))
        ]
        for copy in copies:
            copy.start()
        for d, copy in enumerate(copies):
            copy.wait_recv()
            total = total + later_in[r, d + 1]
        later += copies
    entries = sections * 2 * rows_own * 2 * half
    root_mean = jnp.sqrt(total / entries + 1e-06)
    scale[...] = jnp.broadcast_to(jnp.minimum(1.0, CLIP_LEVEL / root_mean), scale.shape)

    for copy in firsts + later:
        copy.wait_send()


def finish(updated, compensated, scale, gout, eout, scaled, sem):
    half = scaled.shape[2]
    core = lax.axis_index("expert")
    copies = [pltpu.make_async_copy(updated, gout, sem.at[0])]
    copies[0].start()
    factor = scale[0:1, 0:1]
    for side, here in ((0, core), (1, 1 - core)):
        scaled[side] = (compensated[side] * factor).astype(BF16)
        cols = pl.ds(pl.multiple_of(here * half, 128), half)
        copies.append(pltpu.make_async_copy(scaled.at[side], eout.at[:, cols], sem.at[side + 1]))
        copies[-1].start()
    for copy in copies:
        copy.wait()


def per_device(incoming, expert_ids, gates, pre_act, w_up, w_down, delta, w_router):
    sections = lax.axis_size("section")
    steps = expert_ids.shape[0]
    tokens, half = incoming.shape
    local_experts, hidden_units, features = w_up.shape
    slots = pre_act.shape[1]
    rows_own = local_experts * hidden_units
    width = 2 * rows_own
    strides = round_strides(sections)
    rounds = max(1, len(strides))
    group = min(RADIX, sections)
    flat = (rows_own, features)
    vmem = pl.BlockSpec(memory_space=pltpu.VMEM)
    hbm = pl.BlockSpec(memory_space=pltpu.HBM)
    dma = pltpu.SemaphoreType.DMA
    updated, compensated, scale = pl.pallas_call(
        functools.partial(kernel, sections, slots // local_experts),
        out_shape=(
            jax.ShapeDtypeStruct((tokens, half), BF16),
            jax.ShapeDtypeStruct((2, rows_own, half), F32),
            jax.ShapeDtypeStruct((8, 128), F32),
        ),
        in_specs=[hbm] * 8,
        out_specs=(vmem, vmem, vmem),
        scratch_shapes=[
            pltpu.VMEM((steps, tokens, half), BF16),
            pltpu.VMEM((steps, tokens, half), BF16),
            pltpu.VMEM((steps - 1, tokens, half), BF16),
            pltpu.VMEM((width, half), BF16),
            pltpu.VMEM((2 * width, half), BF16),
            pltpu.VMEM(flat, BF16),
            pltpu.VMEM((steps, hidden_units, slots), BF16),
            pltpu.VMEM((steps, tokens, width), F32),
            pltpu.VMEM((steps, tokens, width), F32),
            pltpu.VMEM((steps, tokens, width), F32),
            pltpu.VMEM((steps, tokens, width), F32),
            pltpu.VMEM((steps, tokens, width), F32),
            pltpu.VMEM((steps // 2, width, 2 * tokens), BF16),
            pltpu.VMEM((1, 128), F32),
            pltpu.VMEM((2 * group, 1, 128), F32),
            pltpu.VMEM((rounds, RADIX, 1, 128), F32),
            pltpu.VMEM((rounds, 1, 128), F32),
            dma((8,)),
            dma((3,)),
            dma((3,)),
            dma((steps, CHUNKS)),
            dma((steps, CHUNKS)),
            dma((steps, CHUNKS)),
            dma((steps, CHUNKS)),
            dma((steps - 1, CHUNKS)),
            dma((steps - 1, CHUNKS)),
            dma((2 * group,)),
            dma((2 * group,)),
            dma((rounds, RADIX)),
            dma((rounds, RADIX)),
            pltpu.SemaphoreType.REGULAR((max(1, (sections - 1).bit_length()),)),
            pltpu.VMEM((width, width), BF16),
            pltpu.VMEM((steps, 2, tokens), jnp.int32),
            pltpu.VMEM((steps, 2, tokens), F32),
            pltpu.VMEM((steps, hidden_units, slots), BF16),
            pltpu.VMEM((w_router.shape[2], half), BF16),
        ],
        compiler_params=pltpu.CompilerParams(
            collective_id=0, has_side_effects=True, vmem_limit_bytes=40 * 1024 * 1024
        ),
        name="relay",
    )(
        *[pltpu.with_memory_space_constraint(x, pltpu.HBM) for x in (
        incoming,
        expert_ids.transpose(0, 2, 1),
        gates.transpose(0, 2, 1),
        pre_act.transpose(0, 2, 1),
        w_up.reshape(flat),
        w_down.reshape(flat),
        delta.reshape(flat),
        w_router[0].T,
        )]
    )
    grad_out, expert_grad = pl.pallas_call(
        finish,
        out_shape=(
            jax.ShapeDtypeStruct((tokens, half), BF16),
            jax.ShapeDtypeStruct(flat, BF16),
        ),
        in_specs=[vmem, vmem, vmem],
        out_specs=(hbm, hbm),
        scratch_shapes=[pltpu.VMEM((2, rows_own, half), BF16), dma((3,))],
        compiler_params=pltpu.CompilerParams(vmem_limit_bytes=8 * 1024 * 1024),
        name="finish",
    )(updated, compensated, scale)
    return (grad_out, expert_grad.reshape(w_down.shape))


def solution(mesh):
    return jax.shard_map(
        per_device,
        mesh=mesh,
        in_specs=(
            P("section", "expert"),
            P(None, "section", None),
            P(None, "section", None),
            P(None, ("section", "expert"), None),
            P(("section", "expert"), None, None),
            P(("section", "expert"), None, None),
            P(("section", "expert"), None, None),
            P("section", "expert", None),
        ),
        out_specs=(P("section", "expert"), P(("section", "expert"), None, None)),
        check_vma=False,
    )
```

```python
import functools

import jax
import jax.numpy as jnp
from jax import lax
from jax.experimental import pallas as pl
from jax.experimental.pallas import tpu as pltpu
from jax.sharding import PartitionSpec as P

COMPENSATION = 0.5
CLIP_LEVEL = 1.0
BLOCKS = (4, 4, 4, 2)
CHUNKS = 4
LESSONS = ((), ((0, 0, 1), (2, 1, 2)), ((0, 2, 3), (2, 3, 4)), ((0, 4, 32),))
PIECES = 4
RADIX = 16
F32 = jnp.float32
BF16 = jnp.bfloat16


def dot(a, b):
    return lax.dot_general(a, b, (((1,), (0,)), ((), ())), preferred_element_type=F32)


def dot_nt(a, b):
    return lax.dot_general(a, b, (((1,), (1,)), ((), ())), preferred_element_type=F32)


def ones_where(mask):
    return jnp.where(mask, 1.0, 0.0).astype(BF16)


def round_strides(sections):
    strides = []
    stride = min(RADIX, sections)
    while stride < sections:
        strides.append(stride)
        stride *= min(RADIX, sections // stride)
    return strides


def kernel(
    sections,
    capacity,
    inc,
    ids_hbm,
    gates_hbm,
    pre_hbm,
    wup,
    wdn,
    delta,
    wr_hbm,
    gout,
    acc,
    scale,
    cur,
    cur_o,
    upd,
    wd,
    wcat,
    dl,
    pre_o,
    p_own,
    p_in,
    hid,
    slope,
    gexp,
    hgt,
    mine,
    first_in,
    later_in,
    later_out,
    local_sem,
    w_send,
    w_recv,
    p_send,
    p_recv,
    o_send,
    o_recv,
    r_send,
    r_recv,
    f_send,
    f_recv,
    l_send,
    l_recv,
    entered,
    same,
    ids,
    gates,
    pre,
    wr,
):
    steps, tokens, half = cur.shape
    width = wd.shape[0]
    rows_own = wdn.shape[0]
    hidden_units = pre.shape[1]
    slots = pre.shape[2]
    own_experts = slots // capacity
    shift_bits = hidden_units.bit_length() - 1
    chunk = tokens // CHUNKS
    piece = half // PIECES
    core = lax.axis_index("expert")
    other = 1 - core
    section = lax.axis_index("section")
    is_last = section == sections - 1
    partner = {"section": section, "expert": other}
    group = min(RADIX, sections)
    strides = round_strides(sections)

    below = {"section": jnp.maximum(section - 1, 0), "expert": core}

    def group_peer(d):
        place = (section % group) * 2 + core
        place = (place + d) % (2 * group)
        return {"section": section - section % group + place // 2, "expert": place % 2}

    def later_peer(stride, d):
        size = min(RADIX, sections // stride)
        digit = (section // stride) % size
        moved = (digit + d) % size
        return {"section": section + (moved - digit) * stride, "expert": core}

    own_cols = pl.ds(pl.multiple_of(core * half, 128), half)
    other_cols = pl.ds(pl.multiple_of(other * half, 128), half)
    own_rows = pl.ds(pl.multiple_of(core * rows_own, rows_own), rows_own)

    above = {"section": jnp.minimum(section + 1, sections - 1), "expert": core}
    barrier = pltpu.get_barrier_semaphore()

    def signal(sem, peer):
        pl.semaphore_signal(sem, inc=1, device_id=peer, device_id_type=pl.DeviceIdType.MESH)

    signal(barrier, partner)

    @pl.when(jnp.logical_not(is_last))
    def _():
        signal(barrier, above)

    local = [
        pltpu.make_async_copy(inc, cur.at[0], local_sem.at[0]),
        pltpu.make_async_copy(wdn.at[:, own_cols], wd.at[own_rows, :], local_sem.at[1]),
        pltpu.make_async_copy(wup.at[:, own_cols], wcat.at[own_rows, :], local_sem.at[2]),
        pltpu.make_async_copy(delta, dl, local_sem.at[3]),
        pltpu.make_async_copy(ids_hbm, ids, local_sem.at[4]),
        pltpu.make_async_copy(gates_hbm, gates, local_sem.at[5]),
        pltpu.make_async_copy(pre_hbm, pre, local_sem.at[6]),
        pltpu.make_async_copy(wr_hbm, wr, local_sem.at[7]),
    ]
    for copy in local:
        copy.start()

    def remote(src, dst, send, recv, device):
        return pltpu.make_async_remote_copy(
            src_ref=src,
            dst_ref=dst,
            send_sem=send,
            recv_sem=recv,
            device_id=device,
            device_id_type=pl.DeviceIdType.MESH,
        )

    pl.semaphore_wait(barrier, 1 + jnp.where(section > 0, 1, 0))

    known = max(1, (sections - 1).bit_length())

    def tell(r):
        hop = 1 << r

        @pl.when(section >= hop)
        def _():
            signal(entered.at[r], {"section": jnp.maximum(section - hop, 0), "expert": core})

        @pl.when(section + hop < sections)
        def _():
            signal(entered.at[r], {"section": jnp.minimum(section + hop, sections - 1), "expert": core})

    def hear(r):
        hop = 1 << r
        heard = jnp.where(section >= hop, 1, 0) + jnp.where(section + hop < sections, 1, 0)
        pl.semaphore_wait(entered.at[r], heard)

    def learn(low, high):
        for r in range(low, min(high, known)):
            if r:
                hear(r - 1)
            tell(r)

    weights = [
        remote(wdn.at[:, other_cols], wd.at[own_rows, :], w_send.at[1], w_recv.at[1], partner),
        remote(pre_hbm, pre_o, w_send.at[0], w_recv.at[0], partner),
        remote(wup.at[:, other_cols], wcat.at[own_rows, :], w_send.at[2], w_recv.at[2], partner),
    ]
    for copy in weights:
        copy.start()

    for k in range(1, steps):

        @pl.when(section + k >= sections)
        def _():
            cur[k] = jnp.zeros((tokens, half), BF16)

    def rows_of(q, size):
        return pl.ds(pl.multiple_of(q * size, size), size)

    def p_copy(k, q):
        rows = rows_of(q, tokens // BLOCKS[k])
        return remote(p_own.at[k, rows, :], p_in.at[k, rows, :], p_send.at[k, q], p_recv.at[k, q], partner)

    def o_copy(k, q):
        rows = rows_of(q, tokens // BLOCKS[k])
        return remote(cur.at[k, rows, :], cur_o.at[k, rows, :], o_send.at[k, q], o_recv.at[k, q], partner)

    first_o = remote(inc, cur_o.at[0], o_send.at[0, 0], o_recv.at[0, 0], partner)

    def relay(k, i):
        rows = rows_of(i, chunk)
        return remote(upd.at[k, rows, :], cur.at[k + 1, rows, :], r_send.at[k, i], r_recv.at[k, i], below)

    unit_row = lax.broadcasted_iota(jnp.int32, (width, tokens), 0)
    expert = lax.shift_right_logical(unit_row, shift_bits)
    head = (unit_row & (hidden_units - 1)) == 0

    def spread(router):
        row = lax.broadcasted_iota(jnp.int32, (width, router.shape[0]), 0)
        col = lax.broadcasted_iota(jnp.int32, (width, router.shape[0]), 1)
        return dot(ones_where(row == col * hidden_units), router[...]).astype(BF16)

    def fill_constants():
        a = lax.broadcasted_iota(jnp.int32, (width, width), 0)
        b = lax.broadcasted_iota(jnp.int32, (width, width), 1)
        same[...] = ones_where(
            lax.shift_right_logical(a, shift_bits) == lax.shift_right_logical(b, shift_bits)
        )
        wcat[width:, :] = spread(wr)

    def block_diagonal(pre_block, start):
        row = lax.broadcasted_iota(jnp.int32, (width, hidden_units), 0)
        unit = lax.broadcasted_iota(jnp.int32, (width, hidden_units), 1)
        tiled = dot(ones_where((row & (hidden_units - 1)) == unit), pre_block)
        row = lax.broadcasted_iota(jnp.int32, (width, slots), 0)
        col = lax.broadcasted_iota(jnp.int32, (width, slots), 1)
        low = (lax.shift_right_logical(row, shift_bits) - start) * capacity
        return jnp.where((col >= low) & (col < low + capacity), tiled, 0.0).astype(BF16)

    def prepare(k):
        routing = ids[k]
        gate_vals = gates[k]
        id0, id1 = routing[0:1, :], routing[1:2, :]
        g0, g1 = gate_vals[0:1, :], gate_vals[1:2, :]
        on0, on1 = id0 == expert, id1 == expert
        gate = jnp.where(on0, g0, jnp.where(on1, g1, 0.0))
        row = lax.broadcasted_iota(jnp.int32, (tokens, tokens), 0)
        col = lax.broadcasted_iota(jnp.int32, (tokens, tokens), 1)
        slot = dot(ones_where(on0 | on1), ones_where(row < col))
        slot0 = jnp.sum(jnp.where(on0 & head, slot, 0.0), axis=0, keepdims=True)
        slot1 = jnp.sum(jnp.where(on1 & head, slot, 0.0), axis=0, keepdims=True)
        place0 = id0 * capacity + slot0.astype(jnp.int32)
        place1 = id1 * capacity + slot1.astype(jnp.int32)
        at = lax.broadcasted_iota(jnp.int32, (slots, tokens), 0)
        act = jnp.zeros((width, tokens), F32)
        for ref, side in ((pre, core), (pre_o, other)):
            start = side * own_experts
            here = at + start * capacity
            picked = ones_where((here == place0) | (here == place1))
            act = act + dot(block_diagonal(ref[k], start), picked)
        sig = 1.0 / (1.0 + jnp.exp(-act))
        hidden = (act * sig).astype(BF16).astype(F32)
        hgt[k // 2, :, pl.ds(k % 2 * tokens, tokens)] = (hidden * gate).astype(BF16)
        hid[k] = jnp.transpose(hidden)
        slope[k] = jnp.transpose(sig * (1.0 + act * (1.0 - sig)) * gate)
        gexp[k] = jnp.transpose(gate)

    def stage_a(k, q):
        rows = rows_of(q, tokens // BLOCKS[k])
        p_own[k, rows, :] = dot_nt(cur[k, rows, :], wd[...])
        p_copy(k, q).start()

    def coefficients(k, q):
        rows = rows_of(q, tokens // BLOCKS[k])
        p_copy(k, q).wait_recv()
        total = p_own[k, rows, :] + p_in[k, rows, :]
        hidden = hid[k, rows, :]
        gate = gexp[k, rows, :]
        product = hidden * total
        high = product.astype(BF16)
        low = (product - high.astype(F32)).astype(BF16)
        summed = same[...]
        gate_grad = dot(high, summed) + dot(low, summed)
        mean = jnp.sum(gate * product, axis=1, keepdims=True)
        logit = (gate * (gate_grad - mean)).astype(BF16)
        act = (slope[k, rows, :] * total).astype(BF16)
        both = jnp.concatenate([act, logit], axis=1)
        return both

    def advance(base, both, table, rows, put):
        for n in range(PIECES):
            cols = pl.ds(n * piece, piece)
            value = base[rows, cols].astype(F32) + dot(both, table[:, cols])
            put(cols, value.astype(BF16))

    def stage_b(k, q):
        rows = rows_of(q, tokens // BLOCKS[k])
        both = coefficients(k, q)

        def put(cols, value):
            if k == steps - 1:
                gout[rows, cols] = value
            else:
                upd[k, rows, cols] = value

        advance(cur.at[k], both, wcat, rows, put)
        if k == steps - 1:
            return
        per = CHUNKS // BLOCKS[k]

        @pl.when((section > 0) & (section + k < sections))
        def _():
            for j in range(per):
                relay(k, q * per + j).start()

    def arrive(k, q):
        per = CHUNKS // BLOCKS[k]

        @pl.when(section + k < sections)
        def _():
            for j in range(per):
                relay(k - 1, q * per + j).wait_recv()

        o_copy(k, q).start()

    def weight_piece(pair, n, side):
        cols = pl.ds(pl.multiple_of(n * piece, 128), piece)
        ref = cur_o if side else cur
        block = ref[2 * pair : 2 * pair + 2, :, cols].reshape(2 * tokens, piece)
        return dot(hgt[pair, own_rows, :], block)

    def loop(body, count):
        def step(q, carry):
            body(q)
            return carry

        lax.fori_loop(0, count, step, 0)

    local[0].wait()
    local[1].wait()
    weights[0].wait_recv()
    p_own[0] = dot_nt(cur[0], wd[...])
    loop(lambda q: p_copy(0, q).start(), BLOCKS[0])
    for copy in local[4:]:
        copy.wait()
    weights[1].wait_recv()
    fill_constants()
    prepare(0)
    local[2].wait()
    weights[2].wait_recv()
    loop(lambda q: stage_b(0, q), BLOCKS[0])

    first_o.start()
    for k in range(1, steps):
        prepare(k)

    def early(n):
        cols = pl.ds(pl.multiple_of(n * piece, 128), piece)
        for side in (0, 1):
            acc[side, :, cols] = weight_piece(0, n, side)

    def middle(k):
        def body(q):
            arrive(k, q)
            stage_a(k, q)
            stage_b(k, q)
            for at, low, high in LESSONS[k]:

                @pl.when(q == at)
                def _():
                    learn(low, high)

        return body

    loop(middle(1), BLOCKS[1])
    first_o.wait_recv()
    loop(lambda q: o_copy(1, q).wait_recv(), BLOCKS[1])
    loop(early, PIECES)
    loop(middle(2), BLOCKS[2])
    last = steps - 1
    final = BLOCKS[last] - 1

    loop(middle(last), final)
    local[3].wait()
    arrive(last, final)
    squares = jnp.zeros((1, piece), F32)
    for side, here in ((0, core), (1, other)):
        if side:
            stage_a(last, final)
            for k in (last - 1, last):
                loop(lambda q: o_copy(k, q).wait_recv(), BLOCKS[k])
        for n in range(PIECES):
            cols = pl.ds(n * piece, piece)
            shift = dl[:, pl.ds(pl.multiple_of(here * half + n * piece, 128), piece)].astype(F32)
            grad = acc[side, :, cols] + weight_piece(1, n, side)
            value = grad + COMPENSATION * grad * grad * shift
            acc[side, :, cols] = value
            squares = squares + jnp.sum(value * value, axis=0, keepdims=True)
    hear(known - 1)
    mine[...] = jnp.broadcast_to(jnp.sum(squares, axis=1, keepdims=True), mine.shape)

    firsts = [
        remote(mine, first_in.at[d], f_send.at[d], f_recv.at[d], group_peer(d))
        for d in range(1, 2 * group)
    ]
    for copy in firsts:
        copy.start()
    stage_b(last, final)
    for copy in weights + [first_o]:
        copy.wait_send()

    for k in range(last):

        @pl.when((section > 0) & (section + k < sections))
        def _():
            loop(lambda i: relay(k, i).wait_send(), CHUNKS)

    for k in range(steps):
        loop(lambda q: p_copy(k, q).wait_send(), BLOCKS[k])
        if k:
            loop(lambda q: o_copy(k, q).wait_send(), BLOCKS[k])

    total = mine[...]
    for d, copy in enumerate(firsts):
        copy.wait_recv()
        total = total + first_in[d + 1]
    later = []
    for r, stride in enumerate(strides):
        later_out[r] = total
        copies = [
            remote(
                later_out.at[r],
                later_in.at[r, d],
                l_send.at[r, d],
                l_recv.at[r, d],
                later_peer(stride, d),
            )
            for d in range(1, min(RADIX, sections // stride))
        ]
        for copy in copies:
            copy.start()
        for d, copy in enumerate(copies):
            copy.wait_recv()
            total = total + later_in[r, d + 1]
        later += copies
    entries = sections * 2 * rows_own * 2 * half
    root_mean = jnp.sqrt(total / entries + 1e-06)
    scale[...] = jnp.broadcast_to(jnp.minimum(1.0, CLIP_LEVEL / root_mean), scale.shape)

    for copy in firsts + later:
        copy.wait_send()


def finish(updated, compensated, scale, gout, eout, scaled, sem):
    half = scaled.shape[2]
    core = lax.axis_index("expert")
    copies = [pltpu.make_async_copy(updated, gout, sem.at[0])]
    copies[0].start()
    factor = scale[0:1, 0:1]
    for side, here in ((0, core), (1, 1 - core)):
        scaled[side] = (compensated[side] * factor).astype(BF16)
        cols = pl.ds(pl.multiple_of(here * half, 128), half)
        copies.append(pltpu.make_async_copy(scaled.at[side], eout.at[:, cols], sem.at[side + 1]))
        copies[-1].start()
    for copy in copies:
        copy.wait()


def per_device(incoming, expert_ids, gates, pre_act, w_up, w_down, delta, w_router):
    sections = lax.axis_size("section")
    steps = expert_ids.shape[0]
    tokens, half = incoming.shape
    local_experts, hidden_units, features = w_up.shape
    slots = pre_act.shape[1]
    rows_own = local_experts * hidden_units
    width = 2 * rows_own
    strides = round_strides(sections)
    rounds = max(1, len(strides))
    group = min(RADIX, sections)
    flat = (rows_own, features)
    vmem = pl.BlockSpec(memory_space=pltpu.VMEM)
    hbm = pl.BlockSpec(memory_space=pltpu.HBM)
    dma = pltpu.SemaphoreType.DMA
    updated, compensated, scale = pl.pallas_call(
        functools.partial(kernel, sections, slots // local_experts),
        out_shape=(
            jax.ShapeDtypeStruct((tokens, half), BF16),
            jax.ShapeDtypeStruct((2, rows_own, half), F32),
            jax.ShapeDtypeStruct((8, 128), F32),
        ),
        in_specs=[hbm] * 8,
        out_specs=(vmem, vmem, vmem),
        scratch_shapes=[
            pltpu.VMEM((steps, tokens, half), BF16),
            pltpu.VMEM((steps, tokens, half), BF16),
            pltpu.VMEM((steps - 1, tokens, half), BF16),
            pltpu.VMEM((width, half), BF16),
            pltpu.VMEM((2 * width, half), BF16),
            pltpu.VMEM(flat, BF16),
            pltpu.VMEM((steps, hidden_units, slots), BF16),
            pltpu.VMEM((steps, tokens, width), F32),
            pltpu.VMEM((steps, tokens, width), F32),
            pltpu.VMEM((steps, tokens, width), F32),
            pltpu.VMEM((steps, tokens, width), F32),
            pltpu.VMEM((steps, tokens, width), F32),
            pltpu.VMEM((steps // 2, width, 2 * tokens), BF16),
            pltpu.VMEM((1, 128), F32),
            pltpu.VMEM((2 * group, 1, 128), F32),
            pltpu.VMEM((rounds, RADIX, 1, 128), F32),
            pltpu.VMEM((rounds, 1, 128), F32),
            dma((8,)),
            dma((3,)),
            dma((3,)),
            dma((steps, CHUNKS)),
            dma((steps, CHUNKS)),
            dma((steps, CHUNKS)),
            dma((steps, CHUNKS)),
            dma((steps - 1, CHUNKS)),
            dma((steps - 1, CHUNKS)),
            dma((2 * group,)),
            dma((2 * group,)),
            dma((rounds, RADIX)),
            dma((rounds, RADIX)),
            pltpu.SemaphoreType.REGULAR((max(1, (sections - 1).bit_length()),)),
            pltpu.VMEM((width, width), BF16),
            pltpu.VMEM((steps, 2, tokens), jnp.int32),
            pltpu.VMEM((steps, 2, tokens), F32),
            pltpu.VMEM((steps, hidden_units, slots), BF16),
            pltpu.VMEM((w_router.shape[2], half), BF16),
        ],
        compiler_params=pltpu.CompilerParams(
            collective_id=0, has_side_effects=True, vmem_limit_bytes=40 * 1024 * 1024
        ),
        name="relay",
    )(
        *[pltpu.with_memory_space_constraint(x, pltpu.HBM) for x in (
        incoming,
        expert_ids.transpose(0, 2, 1),
        gates.transpose(0, 2, 1),
        pre_act.transpose(0, 2, 1),
        w_up.reshape(flat),
        w_down.reshape(flat),
        delta.reshape(flat),
        w_router[0].T,
        )]
    )
    grad_out, expert_grad = pl.pallas_call(
        finish,
        out_shape=(
            jax.ShapeDtypeStruct((tokens, half), BF16),
            jax.ShapeDtypeStruct(flat, BF16),
        ),
        in_specs=[vmem, vmem, vmem],
        out_specs=(hbm, hbm),
        scratch_shapes=[pltpu.VMEM((2, rows_own, half), BF16), dma((3,))],
        compiler_params=pltpu.CompilerParams(vmem_limit_bytes=8 * 1024 * 1024),
        name="finish",
    )(updated, compensated, scale)
    return (grad_out, expert_grad.reshape(w_down.shape))


def solution(mesh):
    return jax.shard_map(
        per_device,
        mesh=mesh,
        in_specs=(
            P("section", "expert"),
            P(None, "section", None),
            P(None, "section", None),
            P(None, ("section", "expert"), None),
            P(("section", "expert"), None, None),
            P(("section", "expert"), None, None),
            P(("section", "expert"), None, None),
            P("section", "expert", None),
        ),
        out_specs=(P("section", "expert"), P(("section", "expert"), None, None)),
        check_vma=False,
    )
```

```python
import functools

import jax
import jax.numpy as jnp
from jax import lax
from jax.experimental import pallas as pl
from jax.experimental.pallas import tpu as pltpu
from jax.sharding import PartitionSpec as P

COMPENSATION = 0.5
CLIP_LEVEL = 1.0
BLOCKS = (4, 4, 4, 4)
CHUNKS = 4
LESSONS = ((), ((0, 0, 1), (2, 1, 2)), ((0, 2, 3), (2, 3, 4)), ((0, 4, 32),))
PIECES = 4
RADIX = 16
F32 = jnp.float32
BF16 = jnp.bfloat16


def dot(a, b):
    return lax.dot_general(a, b, (((1,), (0,)), ((), ())), preferred_element_type=F32)


def dot_nt(a, b):
    return lax.dot_general(a, b, (((1,), (1,)), ((), ())), preferred_element_type=F32)


def ones_where(mask):
    return jnp.where(mask, 1.0, 0.0).astype(BF16)


def round_strides(sections):
    strides = []
    stride = min(RADIX, sections)
    while stride < sections:
        strides.append(stride)
        stride *= min(RADIX, sections // stride)
    return strides


def kernel(
    sections,
    capacity,
    inc,
    ids_hbm,
    gates_hbm,
    pre_hbm,
    wup,
    wdn,
    delta,
    wr_hbm,
    gout,
    acc,
    scale,
    cur,
    cur_o,
    upd,
    wd,
    wcat,
    dl,
    pre_o,
    p_own,
    p_in,
    hid,
    slope,
    gexp,
    hgt,
    mine,
    first_in,
    later_in,
    later_out,
    local_sem,
    w_send,
    w_recv,
    p_send,
    p_recv,
    o_send,
    o_recv,
    r_send,
    r_recv,
    f_send,
    f_recv,
    l_send,
    l_recv,
    entered,
    same,
    ids,
    gates,
    pre,
    wr,
):
    steps, tokens, half = cur.shape
    width = wd.shape[0]
    rows_own = wdn.shape[0]
    hidden_units = pre.shape[1]
    slots = pre.shape[2]
    own_experts = slots // capacity
    shift_bits = hidden_units.bit_length() - 1
    chunk = tokens // CHUNKS
    piece = half // PIECES
    core = lax.axis_index("expert")
    other = 1 - core
    section = lax.axis_index("section")
    is_last = section == sections - 1
    partner = {"section": section, "expert": other}
    group = min(RADIX, sections)
    strides = round_strides(sections)

    below = {"section": jnp.maximum(section - 1, 0), "expert": core}

    def group_peer(d):
        place = (section % group) * 2 + core
        place = (place + d) % (2 * group)
        return {"section": section - section % group + place // 2, "expert": place % 2}

    def later_peer(stride, d):
        size = min(RADIX, sections // stride)
        digit = (section // stride) % size
        moved = (digit + d) % size
        return {"section": section + (moved - digit) * stride, "expert": core}

    own_cols = pl.ds(pl.multiple_of(core * half, 128), half)
    other_cols = pl.ds(pl.multiple_of(other * half, 128), half)
    own_rows = pl.ds(pl.multiple_of(core * rows_own, rows_own), rows_own)

    above = {"section": jnp.minimum(section + 1, sections - 1), "expert": core}
    barrier = pltpu.get_barrier_semaphore()

    def signal(sem, peer):
        pl.semaphore_signal(sem, inc=1, device_id=peer, device_id_type=pl.DeviceIdType.MESH)

    signal(barrier, partner)

    @pl.when(jnp.logical_not(is_last))
    def _():
        signal(barrier, above)

    local = [
        pltpu.make_async_copy(inc, cur.at[0], local_sem.at[0]),
        pltpu.make_async_copy(wdn.at[:, own_cols], wd.at[own_rows, :], local_sem.at[1]),
        pltpu.make_async_copy(wup.at[:, own_cols], wcat.at[own_rows, :], local_sem.at[2]),
        pltpu.make_async_copy(delta, dl, local_sem.at[3]),
        pltpu.make_async_copy(ids_hbm, ids, local_sem.at[4]),
        pltpu.make_async_copy(gates_hbm, gates, local_sem.at[5]),
        pltpu.make_async_copy(pre_hbm, pre, local_sem.at[6]),
        pltpu.make_async_copy(wr_hbm, wr, local_sem.at[7]),
    ]
    for copy in local:
        copy.start()

    def remote(src, dst, send, recv, device):
        return pltpu.make_async_remote_copy(
            src_ref=src,
            dst_ref=dst,
            send_sem=send,
            recv_sem=recv,
            device_id=device,
            device_id_type=pl.DeviceIdType.MESH,
        )

    pl.semaphore_wait(barrier, 1 + jnp.where(section > 0, 1, 0))

    known = max(1, (sections - 1).bit_length())

    def tell(r):
        hop = 1 << r

        @pl.when(section >= hop)
        def _():
            signal(entered.at[r], {"section": jnp.maximum(section - hop, 0), "expert": core})

        @pl.when(section + hop < sections)
        def _():
            signal(entered.at[r], {"section": jnp.minimum(section + hop, sections - 1), "expert": core})

    def hear(r):
        hop = 1 << r
        heard = jnp.where(section >= hop, 1, 0) + jnp.where(section + hop < sections, 1, 0)
        pl.semaphore_wait(entered.at[r], heard)

    def learn(low, high):
        for r in range(low, min(high, known)):
            if r:
                hear(r - 1)
            tell(r)

    weights = [
        remote(wdn.at[:, other_cols], wd.at[own_rows, :], w_send.at[1], w_recv.at[1], partner),
        remote(pre_hbm, pre_o, w_send.at[0], w_recv.at[0], partner),
        remote(wup.at[:, other_cols], wcat.at[own_rows, :], w_send.at[2], w_recv.at[2], partner),
    ]
    for copy in weights:
        copy.start()

    for k in range(1, steps):

        @pl.when(section + k >= sections)
        def _():
            cur[k] = jnp.zeros((tokens, half), BF16)

    def rows_of(q, size):
        return pl.ds(pl.multiple_of(q * size, size), size)

    def p_copy(k, q):
        rows = rows_of(q, tokens // BLOCKS[k])
        return remote(p_own.at[k, rows, :], p_in.at[k, rows, :], p_send.at[k, q], p_recv.at[k, q], partner)

    def o_copy(k, q):
        rows = rows_of(q, tokens // BLOCKS[k])
        return remote(cur.at[k, rows, :], cur_o.at[k, rows, :], o_send.at[k, q], o_recv.at[k, q], partner)

    first_o = remote(inc, cur_o.at[0], o_send.at[0, 0], o_recv.at[0, 0], partner)

    def relay(k, i):
        rows = rows_of(i, chunk)
        return remote(upd.at[k, rows, :], cur.at[k + 1, rows, :], r_send.at[k, i], r_recv.at[k, i], below)

    unit_row = lax.broadcasted_iota(jnp.int32, (width, tokens), 0)
    expert = lax.shift_right_logical(unit_row, shift_bits)
    head = (unit_row & (hidden_units - 1)) == 0

    def spread(router):
        row = lax.broadcasted_iota(jnp.int32, (width, router.shape[0]), 0)
        col = lax.broadcasted_iota(jnp.int32, (width, router.shape[0]), 1)
        return dot(ones_where(row == col * hidden_units), router[...]).astype(BF16)

    def fill_constants():
        a = lax.broadcasted_iota(jnp.int32, (width, width), 0)
        b = lax.broadcasted_iota(jnp.int32, (width, width), 1)
        same[...] = ones_where(
            lax.shift_right_logical(a, shift_bits) == lax.shift_right_logical(b, shift_bits)
        )
        wcat[width:, :] = spread(wr)

    def block_diagonal(pre_block, start):
        row = lax.broadcasted_iota(jnp.int32, (width, hidden_units), 0)
        unit = lax.broadcasted_iota(jnp.int32, (width, hidden_units), 1)
        tiled = dot(ones_where((row & (hidden_units - 1)) == unit), pre_block)
        row = lax.broadcasted_iota(jnp.int32, (width, slots), 0)
        col = lax.broadcasted_iota(jnp.int32, (width, slots), 1)
        low = (lax.shift_right_logical(row, shift_bits) - start) * capacity
        return jnp.where((col >= low) & (col < low + capacity), tiled, 0.0).astype(BF16)

    def prepare(k):
        routing = ids[k]
        gate_vals = gates[k]
        id0, id1 = routing[0:1, :], routing[1:2, :]
        g0, g1 = gate_vals[0:1, :], gate_vals[1:2, :]
        on0, on1 = id0 == expert, id1 == expert
        gate = jnp.where(on0, g0, jnp.where(on1, g1, 0.0))
        row = lax.broadcasted_iota(jnp.int32, (tokens, tokens), 0)
        col = lax.broadcasted_iota(jnp.int32, (tokens, tokens), 1)
        slot = dot(ones_where(on0 | on1), ones_where(row < col))
        slot0 = jnp.sum(jnp.where(on0 & head, slot, 0.0), axis=0, keepdims=True)
        slot1 = jnp.sum(jnp.where(on1 & head, slot, 0.0), axis=0, keepdims=True)
        place0 = id0 * capacity + slot0.astype(jnp.int32)
        place1 = id1 * capacity + slot1.astype(jnp.int32)
        at = lax.broadcasted_iota(jnp.int32, (slots, tokens), 0)
        act = jnp.zeros((width, tokens), F32)
        for ref, side in ((pre, core), (pre_o, other)):
            start = side * own_experts
            here = at + start * capacity
            picked = ones_where((here == place0) | (here == place1))
            act = act + dot(block_diagonal(ref[k], start), picked)
        sig = 1.0 / (1.0 + jnp.exp(-act))
        hidden = (act * sig).astype(BF16).astype(F32)
        hgt[k // 2, :, pl.ds(k % 2 * tokens, tokens)] = (hidden * gate).astype(BF16)
        hid[k] = jnp.transpose(hidden)
        slope[k] = jnp.transpose(sig * (1.0 + act * (1.0 - sig)) * gate)
        gexp[k] = jnp.transpose(gate)

    def stage_a(k, q):
        rows = rows_of(q, tokens // BLOCKS[k])
        p_own[k, rows, :] = dot_nt(cur[k, rows, :], wd[...])
        p_copy(k, q).start()

    def coefficients(k, q):
        rows = rows_of(q, tokens // BLOCKS[k])
        p_copy(k, q).wait_recv()
        total = p_own[k, rows, :] + p_in[k, rows, :]
        hidden = hid[k, rows, :]
        gate = gexp[k, rows, :]
        product = hidden * total
        high = product.astype(BF16)
        low = (product - high.astype(F32)).astype(BF16)
        summed = same[...]
        gate_grad = dot(high, summed) + dot(low, summed)
        mean = jnp.sum(gate * product, axis=1, keepdims=True)
        logit = (gate * (gate_grad - mean)).astype(BF16)
        act = (slope[k, rows, :] * total).astype(BF16)
        both = jnp.concatenate([act, logit], axis=1)
        return both

    def advance(base, both, table, rows, put):
        for n in range(PIECES):
            cols = pl.ds(n * piece, piece)
            value = base[rows, cols].astype(F32) + dot(both, table[:, cols])
            put(cols, value.astype(BF16))

    def stage_b(k, q):
        rows = rows_of(q, tokens // BLOCKS[k])
        both = coefficients(k, q)

        def put(cols, value):
            if k == steps - 1:
                gout[rows, cols] = value
            else:
                upd[k, rows, cols] = value

        advance(cur.at[k], both, wcat, rows, put)
        if k == steps - 1:
            return
        per = CHUNKS // BLOCKS[k]

        @pl.when((section > 0) & (section + k < sections))
        def _():
            for j in range(per):
                relay(k, q * per + j).start()

    def arrive(k, q):
        per = CHUNKS // BLOCKS[k]

        @pl.when(section + k < sections)
        def _():
            for j in range(per):
                relay(k - 1, q * per + j).wait_recv()

        o_copy(k, q).start()

    def weight_piece(pair, n, side):
        cols = pl.ds(pl.multiple_of(n * piece, 128), piece)
        ref = cur_o if side else cur
        block = ref[2 * pair : 2 * pair + 2, :, cols].reshape(2 * tokens, piece)
        return dot(hgt[pair, own_rows, :], block)

    def loop(body, count):
        def step(q, carry):
            body(q)
            return carry

        lax.fori_loop(0, count, step, 0)

    for copy in local[4:]:
        copy.wait()
    fill_constants()
    local[0].wait()
    local[1].wait()
    weights[0].wait_recv()
    p_own[0] = dot_nt(cur[0], wd[...])
    loop(lambda q: p_copy(0, q).start(), BLOCKS[0])
    weights[1].wait_recv()
    prepare(0)
    local[2].wait()
    weights[2].wait_recv()
    loop(lambda q: stage_b(0, q), BLOCKS[0])

    first_o.start()
    for k in range(1, steps):
        prepare(k)

    def early(n):
        cols = pl.ds(pl.multiple_of(n * piece, 128), piece)
        for side in (0, 1):
            acc[side, :, cols] = weight_piece(0, n, side)

    def middle(k):
        def body(q):
            arrive(k, q)
            stage_a(k, q)
            stage_b(k, q)
            for at, low, high in LESSONS[k]:

                @pl.when(q == at)
                def _():
                    learn(low, high)

        return body

    loop(middle(1), BLOCKS[1])
    first_o.wait_recv()
    loop(lambda q: o_copy(1, q).wait_recv(), BLOCKS[1])
    loop(early, PIECES)
    loop(middle(2), BLOCKS[2])
    last = steps - 1
    final = BLOCKS[last] - 1

    loop(middle(last), final)
    local[3].wait()
    arrive(last, final)
    squares = jnp.zeros((1, piece), F32)
    for side, here in ((0, core), (1, other)):
        if side:
            stage_a(last, final)
            for k in (last - 1, last):
                loop(lambda q: o_copy(k, q).wait_recv(), BLOCKS[k])
        for n in range(PIECES):
            cols = pl.ds(n * piece, piece)
            shift = dl[:, pl.ds(pl.multiple_of(here * half + n * piece, 128), piece)].astype(F32)
            grad = acc[side, :, cols] + weight_piece(1, n, side)
            value = grad + COMPENSATION * grad * grad * shift
            acc[side, :, cols] = value
            squares = squares + jnp.sum(value * value, axis=0, keepdims=True)
    hear(known - 1)
    mine[...] = jnp.broadcast_to(jnp.sum(squares, axis=1, keepdims=True), mine.shape)

    firsts = [
        remote(mine, first_in.at[d], f_send.at[d], f_recv.at[d], group_peer(d))
        for d in range(1, 2 * group)
    ]
    for copy in firsts:
        copy.start()
    stage_b(last, final)
    for copy in weights + [first_o]:
        copy.wait_send()

    for k in range(last):

        @pl.when((section > 0) & (section + k < sections))
        def _():
            loop(lambda i: relay(k, i).wait_send(), CHUNKS)

    for k in range(steps):
        loop(lambda q: p_copy(k, q).wait_send(), BLOCKS[k])
        if k:
            loop(lambda q: o_copy(k, q).wait_send(), BLOCKS[k])

    total = mine[...]
    for d, copy in enumerate(firsts):
        copy.wait_recv()
        total = total + first_in[d + 1]
    later = []
    for r, stride in enumerate(strides):
        later_out[r] = total
        copies = [
            remote(
                later_out.at[r],
                later_in.at[r, d],
                l_send.at[r, d],
                l_recv.at[r, d],
                later_peer(stride, d),
            )
            for d in range(1, min(RADIX, sections // stride))
        ]
        for copy in copies:
            copy.start()
        for d, copy in enumerate(copies):
            copy.wait_recv()
            total = total + later_in[r, d + 1]
        later += copies
    entries = sections * 2 * rows_own * 2 * half
    root_mean = jnp.sqrt(total / entries + 1e-06)
    scale[...] = jnp.broadcast_to(jnp.minimum(1.0, CLIP_LEVEL / root_mean), scale.shape)

    for copy in firsts + later:
        copy.wait_send()


def finish(updated, compensated, scale, gout, eout, scaled, sem):
    half = scaled.shape[2]
    core = lax.axis_index("expert")
    copies = [pltpu.make_async_copy(updated, gout, sem.at[0])]
    copies[0].start()
    factor = scale[0:1, 0:1]
    part = half // 2
    for n in range(4):
        side, here = (0, core) if n < 2 else (1, 1 - core)
        src = pl.ds(n % 2 * part, part)
        scaled[side, :, src] = (compensated[side, :, src] * factor).astype(BF16)
        cols = pl.ds(pl.multiple_of(here * half + n % 2 * part, 128), part)
        copies.append(pltpu.make_async_copy(scaled.at[side, :, src], eout.at[:, cols], sem.at[n + 1]))
        copies[-1].start()
    for copy in copies:
        copy.wait()


def per_device(incoming, expert_ids, gates, pre_act, w_up, w_down, delta, w_router):
    sections = lax.axis_size("section")
    steps = expert_ids.shape[0]
    tokens, half = incoming.shape
    local_experts, hidden_units, features = w_up.shape
    slots = pre_act.shape[1]
    rows_own = local_experts * hidden_units
    width = 2 * rows_own
    strides = round_strides(sections)
    rounds = max(1, len(strides))
    group = min(RADIX, sections)
    flat = (rows_own, features)
    vmem = pl.BlockSpec(memory_space=pltpu.VMEM)
    hbm = pl.BlockSpec(memory_space=pltpu.HBM)
    dma = pltpu.SemaphoreType.DMA
    updated, compensated, scale = pl.pallas_call(
        functools.partial(kernel, sections, slots // local_experts),
        out_shape=(
            jax.ShapeDtypeStruct((tokens, half), BF16),
            jax.ShapeDtypeStruct((2, rows_own, half), F32),
            jax.ShapeDtypeStruct((8, 128), F32),
        ),
        in_specs=[hbm] * 8,
        out_specs=(vmem, vmem, vmem),
        scratch_shapes=[
            pltpu.VMEM((steps, tokens, half), BF16),
            pltpu.VMEM((steps, tokens, half), BF16),
            pltpu.VMEM((steps - 1, tokens, half), BF16),
            pltpu.VMEM((width, half), BF16),
            pltpu.VMEM((2 * width, half), BF16),
            pltpu.VMEM(flat, BF16),
            pltpu.VMEM((steps, hidden_units, slots), BF16),
            pltpu.VMEM((steps, tokens, width), F32),
            pltpu.VMEM((steps, tokens, width), F32),
            pltpu.VMEM((steps, tokens, width), F32),
            pltpu.VMEM((steps, tokens, width), F32),
            pltpu.VMEM((steps, tokens, width), F32),
            pltpu.VMEM((steps // 2, width, 2 * tokens), BF16),
            pltpu.VMEM((1, 128), F32),
            pltpu.VMEM((2 * group, 1, 128), F32),
            pltpu.VMEM((rounds, RADIX, 1, 128), F32),
            pltpu.VMEM((rounds, 1, 128), F32),
            dma((8,)),
            dma((3,)),
            dma((3,)),
            dma((steps, CHUNKS)),
            dma((steps, CHUNKS)),
            dma((steps, CHUNKS)),
            dma((steps, CHUNKS)),
            dma((steps - 1, CHUNKS)),
            dma((steps - 1, CHUNKS)),
            dma((2 * group,)),
            dma((2 * group,)),
            dma((rounds, RADIX)),
            dma((rounds, RADIX)),
            pltpu.SemaphoreType.REGULAR((max(1, (sections - 1).bit_length()),)),
            pltpu.VMEM((width, width), BF16),
            pltpu.VMEM((steps, 2, tokens), jnp.int32),
            pltpu.VMEM((steps, 2, tokens), F32),
            pltpu.VMEM((steps, hidden_units, slots), BF16),
            pltpu.VMEM((w_router.shape[2], half), BF16),
        ],
        compiler_params=pltpu.CompilerParams(
            collective_id=0, has_side_effects=True, vmem_limit_bytes=40 * 1024 * 1024
        ),
        name="relay",
    )(
        *[pltpu.with_memory_space_constraint(x, pltpu.HBM) for x in (
        incoming,
        expert_ids.transpose(0, 2, 1),
        gates.transpose(0, 2, 1),
        pre_act.transpose(0, 2, 1),
        w_up.reshape(flat),
        w_down.reshape(flat),
        delta.reshape(flat),
        w_router[0].T,
        )]
    )
    grad_out, expert_grad = pl.pallas_call(
        finish,
        out_shape=(
            jax.ShapeDtypeStruct((tokens, half), BF16),
            jax.ShapeDtypeStruct(flat, BF16),
        ),
        in_specs=[vmem, vmem, vmem],
        out_specs=(hbm, hbm),
        scratch_shapes=[pltpu.VMEM((2, rows_own, half), BF16), dma((5,))],
        compiler_params=pltpu.CompilerParams(vmem_limit_bytes=8 * 1024 * 1024),
        name="finish",
    )(updated, compensated, scale)
    return (grad_out, expert_grad.reshape(w_down.shape))


def solution(mesh):
    return jax.shard_map(
        per_device,
        mesh=mesh,
        in_specs=(
            P("section", "expert"),
            P(None, "section", None),
            P(None, "section", None),
            P(None, ("section", "expert"), None),
            P(("section", "expert"), None, None),
            P(("section", "expert"), None, None),
            P(("section", "expert"), None, None),
            P("section", "expert", None),
        ),
        out_specs=(P("section", "expert"), P(("section", "expert"), None, None)),
        check_vma=False,
    )
```
